512 devices in a mesh: clip: 64 (over z, y_hi, x), val: 8 (over y_lo, core).
Axes of the slice: x: 4, y: 8 (y_hi: 2, y_lo: 4; y = y_hi * 4 + y_lo), z: 8, core: 2. Of those that a mesh axis runs over, the one named last changes fastest.
Arguments:
- latents: bfloat16 [1024, 8192], P('clip', 'val'), may hold values from -10 to 10
- noise: bfloat16 [1024, 8192], P('clip', 'val'), may hold values from -10 to 10
- offsets: int32 [1024, 2, 2], P('clip'), may hold values from 0 to 15
- times: float32 [1024], P('clip'), may hold values from 0.05 to 0.95
- embed: bfloat16 [64, 5120], replicated, may hold values from -0.75 to 0.75
Outputs:
- embedded: bfloat16 [1024, 128, 5120], P('clip', 'val')
The draws below stay inside these ranges and needn't reach their ends.
All inputs are finite; a program needn't handle non-finite values.
Results may differ from the reference program's by a relative error of at most 0.0051.
Values may be sent and summed in bfloat16 or wider, within the bound.
A program may use at most 64 MiB of HBM per device.

```python
import math
import jax
import jax.numpy as jnp
from jax import lax

P_SIZE = 64
D = 5120
FR = 2
GW = 16
GH = 4
ITERS = 4
S = 128
N = 1024


def frame_pattern(key, strength_index):
    local_key = jax.random.fold_in(key, 100 + strength_index)
    root_three = math.sqrt(3.0)
    pattern = jax.random.uniform(local_key, (P_SIZE, FR, 1), jnp.float32, -root_three, root_three)
    return jnp.broadcast_to(pattern, (P_SIZE, FR, GH * GW)).reshape(P_SIZE * FR * GH * GW)


def pattern_scale(strength_index):
    target = 150.0 * (strength_index + 1)
    return math.sqrt(target / (2.0 * math.sqrt(P_SIZE * FR * GH * GW)))


def base_rows(key, salt):
    local_key = jax.random.fold_in(key, salt)
    values = jnp.clip(jax.random.normal(local_key, (N, P_SIZE * FR * GH * GW), jnp.float32), -6.0, 6.0)
    return values


def heavy_rows(key):
    local_key = jax.random.fold_in(key, 300)
    values = jnp.clip(3.0 * jax.random.normal(local_key, (2, P_SIZE * FR * GH * GW), jnp.float32), -10.0, 10.0)
    return values


def draw_latents(key, part):
    values = base_rows(key, 1)
    for strength_index in range(3):
        pattern = frame_pattern(key, strength_index)
        values = values.at[strength_index].set(pattern_scale(strength_index) * pattern)
    return values.astype(jnp.bfloat16)


def draw_noise(key, part):
    values = base_rows(key, 2)
    for strength_index in range(3):
        pattern = frame_pattern(key, strength_index)
        scale = pattern_scale(strength_index)
        values = values.at[N - 1 - 2 * strength_index].set(scale * pattern)
        values = values.at[N - 2 - 2 * strength_index].set(1.08 * scale * pattern)
    heavy = heavy_rows(key)
    values = values.at[N // 2 - 2].set(heavy[0])
    values = values.at[N // 2 - 1].set(heavy[1])
    return values.astype(jnp.bfloat16)


def set_ends(values, rng, least, largest):
    longest = values.shape.index(max(values.shape))
    spots = []
    for shift in (0, 1):
        where = [jax.random.randint(jax.random.fold_in(rng, axis), (), 0, length) for axis, length in enumerate(values.shape)]
        where[longest] = (where[longest] + shift) % values.shape[longest]
        spots.append(tuple(where))
    return values.at[spots[0]].set(least).at[spots[1]].set(largest)


def levels(stream_key, shape, split, smallest, high):
    def one(dim, parts):
        steps = jax.random.uniform(jax.random.fold_in(jax.random.fold_in(stream_key, 6), dim), (parts,), jnp.float32, smallest / len(split), high / len(split))
        return jnp.repeat(jnp.exp(steps), shape[dim] // parts).reshape((-1,) + (1,) * (len(shape) - dim - 1))

    loudness = one(*split[0])
    for cut in split[1:]:
        loudness = loudness * one(*cut)
    return loudness


def gaussian(stream_key, dims, spread, limit, kind=jnp.bfloat16):
    entries = jax.random.normal(stream_key, dims, jnp.float32) * spread
    return jnp.minimum(jnp.maximum(entries, -limit), limit).astype(kind)


def setup_inputs(seed: int = 0) -> dict:
    key_of = jax.random.split(jax.random.key(seed), 6)
    latents = draw_latents(jax.random.fold_in(key_of[5], 71), 0)
    noise = draw_noise(jax.random.fold_in(key_of[5], 71), 0)
    offsets = set_ends(jax.random.randint(key_of[2], (N, FR, 2), 0, GW), jax.random.fold_in(key_of[2], 1), 0, GW - 1).astype(jnp.int32)
    times = jnp.clip(0.05 + 0.9 * jax.random.uniform(key_of[3], (N,), jnp.float32) ** levels(key_of[3], (N,), ((0, 64),), -0.2, 0.2), 0.05, 0.95)
    embed = gaussian(key_of[4], (P_SIZE, D), P_SIZE ** -0.5, 0.75)
    return {"latents": latents, "noise": noise, "offsets": offsets, "times": times, "embed": embed}


def warp_noise(noise, offsets):
    clips = noise.shape[0]
    tokens = FR * GH * GW
    value_cube = noise.reshape(clips, noise.shape[1] // tokens, tokens)
    shift_y = offsets[:, :, 0] % GH
    shift_x = offsets[:, :, 1] % GW
    src_rows = (jnp.arange(GH, dtype=jnp.int32)[None, None, :] - shift_y[:, :, None]) % GH
    src_cols = (jnp.arange(GW, dtype=jnp.int32)[None, None, :] - shift_x[:, :, None]) % GW
    frame_base = (jnp.arange(FR, dtype=jnp.int32) * (GH * GW))[None, :, None, None]
    source = (frame_base + src_rows[:, :, :, None] * GW + src_cols[:, :, None, :]).reshape(clips, tokens).astype(jnp.int32)
    source = jnp.broadcast_to(source[:, None, :], value_cube.shape)
    return jnp.take_along_axis(value_cube, source, axis=2).reshape(noise.shape)

def log_sum_exp(values, axis):
    top = lax.optimization_barrier(jnp.max(values, axis=axis, keepdims=True))
    return jnp.squeeze(top + jnp.log(lax.optimization_barrier(jnp.sum(jnp.exp(values - top), axis=axis, keepdims=True))), axis=axis)

def embed_clip(single, embed):
    return jnp.dot(single.T, embed, preferred_element_type=jnp.float32).astype(jnp.bfloat16)

def reference(latents, noise, offsets, times, embed):
    warped = warp_noise(noise, offsets)
    square = lax.optimization_barrier(jnp.sum(jnp.square(warped.astype(jnp.float32)), axis=1))
    gram = jnp.dot(latents, warped.T, preferred_element_type=jnp.float32)
    volume = P_SIZE * S
    cost = (square[None, :] - 2.0 * gram) / volume
    entropy = 0.5 / math.sqrt(volume)
    column_dual = jnp.zeros((N,), jnp.float32)
    for sweep_index in range(ITERS):
        row_dual = -entropy * log_sum_exp((column_dual[None, :] - cost) / entropy, 1)
        column_dual = -entropy * log_sum_exp((row_dual[:, None] - cost) / entropy, 0)
    scores = (column_dual[None, :] - cost) / entropy
    top = lax.optimization_barrier(jnp.max(scores, axis=1, keepdims=True))
    expo = jnp.exp(scores - top)
    weights = (expo / lax.optimization_barrier(jnp.sum(expo, axis=1, keepdims=True))).astype(jnp.bfloat16)
    coupled = jnp.dot(weights, warped, preferred_element_type=jnp.float32)
    mixed = ((1.0 - times)[:, None] * latents.astype(jnp.float32) + times[:, None] * coupled).astype(jnp.bfloat16)
    value_cube = mixed.reshape(N, P_SIZE, S)
    return lax.map(lambda single: embed_clip(single, embed), value_cube)
```

```python
import functools
import math

import jax
import jax.numpy as jnp
from jax import lax
from jax.experimental import pallas as pl
from jax.experimental.pallas import tpu as pltpu
from jax.sharding import PartitionSpec as P

P_SIZE = 64
FR = 2
GW = 16
GH = 4
ITERS = 4
S = FR * GH * GW
LOG2E = 1.4426950408889634


def each(n, step):
    def body(i, carry):
        step(i)
        return carry

    lax.fori_loop(1, n, body, 0)


def couple(nz, nb, nv, lat, noise, off, times, out, wg, lg, part, rv, g, ex, urow, pf, pb, rp, mt, ra,
           w_s, w_r, l_s, l_r, r_s, r_r, g_s, g_r, h_s, h_r, e_s, e_r, c_s, c_r, a_s, a_r):
    nl = nv // 2
    rows, depth = lat.shape
    patches = depth // S
    wide = nz * rows
    st = S // nv
    clip = lax.axis_index("clip")
    v = lax.axis_index("val")
    z, b = clip // nb, lax.rem(clip, nb)
    l, k = v // 2, lax.rem(v, 2)

    def slot(i):
        return lax.rem(i, 2) * nl + i // 2

    def at(z_, b_, v_):
        return {"clip": z_ * nb + b_, "val": v_}

    def along_z(i):
        return at(lax.rem(z + i, nz), b, v)

    def along_b(i):
        return at(z, lax.rem(b + i, nb), v)

    def along_v(i):
        return at(z, b, lax.rem(v + i, nv))

    def send(src, dst, s_sem, r_sem, where):
        return pltpu.make_async_remote_copy(src, dst, s_sem, r_sem, device_id=where)

    barrier = pltpu.get_barrier_semaphore()
    each(nz, lambda i: pl.semaphore_signal(barrier, inc=1, device_id=along_z(i)))
    each(nb, lambda i: pl.semaphore_signal(barrier, inc=1, device_id=along_b(i)))
    each(nv, lambda i: pl.semaphore_signal(barrier, inc=1, device_id=along_v(i)))

    rowi = lax.broadcasted_iota(jnp.int32, (rows, S), 0)
    lane = lax.broadcasted_iota(jnp.int32, (rows, S), 1)
    first = lane < GH * GW
    sy = jnp.zeros((rows, S), jnp.int32)
    sx = jnp.zeros((rows, S), jnp.int32)
    tv = jnp.zeros((rows, S), jnp.float32)
    for i in range(rows):
        here = rowi == i
        sy = jnp.where(here, jnp.where(first, off[i, 0], off[i, 2]), sy)
        sx = jnp.where(here, jnp.where(first, off[i, 1], off[i, 3]), sx)
        tv = jnp.where(here, times[i], tv)
    col = lane & (GW - 1)
    row = (lane // GW) & (GH - 1)
    for p in range(patches):
        x = noise[:, p * S:(p + 1) * S].astype(jnp.float32)
        for bit in (1, 2, 4, 8):
            turned = jnp.where(col >= bit, pltpu.roll(x, bit, 1), pltpu.roll(x, S - GW + bit, 1))
            x = jnp.where((sx & bit) != 0, turned, x)
        for bit in (1, 2):
            turned = jnp.where(
                row >= bit, pltpu.roll(x, bit * GW, 1), pltpu.roll(x, S - GH * GW + bit * GW, 1)
            )
            x = jnp.where((sy & bit) != 0, turned, x)
        wg[z, :, p * S:(p + 1) * S] = x.astype(jnp.bfloat16)
    lg[slot(b)] = lat[...]
    rp[b] = jnp.zeros((rows, depth), jnp.bfloat16)
    pl.semaphore_wait(barrier, (nz - 1) + (nb - 1) + (nv - 1))

    def w_copy(i):
        return send(wg.at[z], wg.at[z], w_s.at[i], w_r.at[z], along_z(i))

    def l_copy(i):
        return send(lat, lg.at[slot(b)], l_s.at[i], l_r.at[b], along_b(i))

    each(nb, lambda i: l_copy(i).start())
    each(nz, lambda i: w_copy(i).start())

    def w_wait(i):
        zt = lax.rem(z + i, nz)
        send(wg.at[zt], wg.at[zt], w_s.at[i], w_r.at[zt], along_z(i)).wait_recv()

    def l_wait(i):
        bt = lax.rem(b + i, nb)
        send(lat, lg.at[slot(bt)], l_s.at[i], l_r.at[bt], along_b(i)).wait_recv()

    each(nz, w_wait)
    panel = wg[...].reshape(wide, depth)
    f32 = panel.astype(jnp.float32)
    square = jnp.sum(f32 * f32, axis=1, keepdims=True)
    diagonal = lax.broadcasted_iota(jnp.int32, (wide, wide), 0) == lax.broadcasted_iota(
        jnp.int32, (wide, wide), 1
    )
    square = jnp.sum(jnp.where(diagonal, square, 0.0), axis=0, keepdims=True)
    each(nb, l_wait)
    gram = lax.dot_general(
        lg[...].reshape(nb * rows, depth), panel, (((1,), (1,)), ((), ())), preferred_element_type=jnp.float32
    )
    part[...] = (square - 2.0 * gram).reshape(nb, rows, wide)

    def r_copy(i):
        vt = lax.rem(v + i, nv)
        return send(part.at[slot(vt)], rv.at[v], r_s.at[i], r_r.at[v], along_v(i))

    each(nv, lambda i: r_copy(i).start())
    rv[v] = part[slot(v)]

    def r_wait(i):
        vt = lax.rem(v + i, nv)
        send(part.at[slot(vt)], rv.at[vt], r_s.at[i], r_r.at[vt], along_v(i)).wait_recv()

    each(nv, r_wait)
    volume = float(nv * depth)
    entropy = 0.5 / math.sqrt(volume)
    mine = pl.ds(pl.multiple_of(b * wide, wide), wide)
    g[k, l, :, mine] = jnp.sum(rv[...], axis=0) * (LOG2E / (volume * entropy))

    n_plane = nl * nb
    own = l * nb + b

    def g_copy(i):
        q = lax.rem(own + i, n_plane)
        here = g.at[k, l, :, mine]
        return send(here, here, g_s.at[i], g_r.at[own], at(z, lax.rem(q, nb), (q // nb) * 2 + k))

    each(n_plane, lambda i: g_copy(i).start())

    def g_wait(i):
        q = lax.rem(own + i, n_plane)
        bt, lt = lax.rem(q, nb), q // nb
        here = g.at[k, lt, :, pl.ds(pl.multiple_of(bt * wide, wide), wide)]
        send(here, here, g_s.at[i], g_r.at[q], at(z, bt, lt * 2 + k)).wait_recv()

    each(n_plane, g_wait)
    other = at(z, b, l * 2 + (1 - k))
    send(g.at[k], g.at[k], h_s, h_r, other).start()
    send(g.at[1 - k], g.at[1 - k], h_s, h_r, other).wait_recv()

    n = nz * nb * rows
    height = nb * rows
    urow[...] = jnp.zeros((1, n), jnp.float32)
    for it in range(ITERS):
        cost = g[...].reshape(height, n)
        t = urow[...] - cost
        top = jnp.max(t, axis=1, keepdims=True)
        total = jnp.sum(jnp.exp2(t - top), axis=1, keepdims=True)
        t = -(top + jnp.log2(total)) - cost
        top = jnp.max(t, axis=0, keepdims=True)
        total = jnp.sum(jnp.exp2(t - top), axis=0, keepdims=True)
        ex[it, z] = top + jnp.log2(total)

        def e_copy(i):
            here = ex.at[it, z]
            return send(here, here, e_s.at[it, i], e_r.at[it, z], along_z(i))

        def e_wait(i):
            zt = lax.rem(z + i, nz)
            here = ex.at[it, zt]
            send(here, here, e_s.at[it, i], e_r.at[it, zt], along_z(i)).wait_recv()

        each(nz, lambda i: e_copy(i).start())
        each(nz, e_wait)
        parts = ex[it]
        top = jnp.max(parts, axis=0)
        total = jnp.sum(jnp.exp2(parts - top[None]), axis=0)
        urow[...] = -(top + jnp.log2(total))

    t = urow[...] - g[...].reshape(height, n)
    top = jnp.max(t, axis=1, keepdims=True)
    total = jnp.sum(jnp.exp2(t - top), axis=1, keepdims=True)
    t = urow[:, mine] - g[:, :, :, mine].reshape(height, wide)
    weights = (jnp.exp2(t - top) / total).astype(jnp.bfloat16)

    coupled = jnp.dot(weights, wg[...].reshape(wide, depth), preferred_element_type=jnp.float32)
    pf[...] = coupled.reshape(nb, rows, depth)
    pb[...] = coupled.astype(jnp.bfloat16).reshape(nb, rows, depth)

    def c_copy(i):
        bt = lax.rem(b + i, nb)
        return send(pb.at[slot(bt)], rp.at[b], c_s.at[i], c_r.at[b], along_b(i))

    def c_wait(i):
        bt = lax.rem(b + i, nb)
        send(pb.at[slot(bt)], rp.at[bt], c_s.at[i], c_r.at[bt], along_b(i)).wait_recv()

    each(nb, lambda i: c_copy(i).start())
    each(nb, c_wait)
    total = pf[slot(b)]
    for j in range(nb):
        total = total + rp[j].astype(jnp.float32)
    tiles = []
    for p in range(patches):
        cut = slice(p * S, (p + 1) * S)
        tiles.append((1.0 - tv) * lat[:, cut].astype(jnp.float32) + tv * total[:, cut])
    mixed = jnp.concatenate(tiles, axis=0)
    mt[...] = mixed.T.astype(jnp.bfloat16).reshape(nv, st, patches * rows)

    def a_copy(i):
        vt = lax.rem(v + i, nv)
        return send(mt.at[vt], ra.at[v], a_s.at[i], a_r.at[v], along_v(i))

    def a_wait(i):
        vt = lax.rem(v + i, nv)
        send(mt.at[vt], ra.at[vt], a_s.at[i], a_r.at[vt], along_v(i)).wait_recv()

    each(nv, lambda i: a_copy(i).start())
    ra[v] = mt[v]
    each(nv, a_wait)
    out[...] = ra[...]

    each(nz, lambda i: w_copy(i).wait_send())
    each(nb, lambda i: l_copy(i).wait_send())
    each(nv, lambda i: r_copy(i).wait_send())
    each(n_plane, lambda i: g_copy(i).wait_send())
    send(g.at[k], g.at[k], h_s, h_r, other).wait_send()
    for it in range(ITERS):
        each(nz, lambda i: send(ex.at[it, z], ex.at[it, z], e_s.at[it, i], e_r.at[it, z], along_z(i)).wait_send())
    each(nb, lambda i: c_copy(i).wait_send())
    each(nv, lambda i: a_copy(i).wait_send())


def embed_tokens(tokens, table, out, x):
    nv, st, width = tokens.shape
    rows = out.shape[0]
    patches = width // rows

    @pl.when(pl.program_id(0) == 0)
    def _():
        clip_of = lax.broadcasted_iota(jnp.int32, (rows, st, width), 0)
        lane = lax.broadcasted_iota(jnp.int32, (rows, st, width), 2)
        keep = (lane & (rows - 1)) == clip_of
        from_lane = lax.broadcasted_iota(jnp.int32, (width, nv * patches), 0) // rows
        to_patch = lax.broadcasted_iota(jnp.int32, (width, nv * patches), 1)
        total = jnp.zeros((rows * st, nv * patches), jnp.float32)
        for j in range(nv):
            spread = jnp.where(keep, tokens[j].astype(jnp.float32)[None], 0.0)
            spread = spread.reshape(rows * st, width).astype(jnp.bfloat16)
            pick = jnp.where(to_patch == from_lane + j * patches, 1.0, 0.0).astype(jnp.bfloat16)
            total = total + jnp.dot(spread, pick, preferred_element_type=jnp.float32)
        x[...] = total.astype(jnp.bfloat16)

    made = jnp.dot(x[...], table[...], preferred_element_type=jnp.float32)
    out[...] = made.astype(jnp.bfloat16).reshape(out.shape)


def on_device(nc, nv, latents, noise, offsets, times, embed):
    nb = nv
    nz = nc // nb
    nl = nv // 2
    rows, depth = latents.shape
    patches = depth // S
    st = S // nv
    wide = nz * rows
    n = nc * rows
    f32, bf16 = jnp.float32, jnp.bfloat16
    dma = pltpu.SemaphoreType.DMA
    vmem = pl.BlockSpec(memory_space=pltpu.VMEM)
    smem = pl.BlockSpec(memory_space=pltpu.SMEM)
    sems = []
    for count in ((nz,), (nb,), (nv,), (nl * nb,), (), (ITERS, nz), (nb,), (nv,)):
        sems += [dma(count), dma(count)]
    tokens = pl.pallas_call(
        functools.partial(couple, nz, nb, nv),
        out_shape=jax.ShapeDtypeStruct((nv, st, patches * rows), bf16),
        in_specs=[vmem, vmem, smem, smem],
        out_specs=vmem,
        scratch_shapes=[
            pltpu.VMEM((nz, rows, depth), bf16),
            pltpu.VMEM((nb, rows, depth), bf16),
            pltpu.VMEM((nb, rows, wide), f32),
            pltpu.VMEM((nv, rows, wide), f32),
            pltpu.VMEM((2, nl, rows, n), f32),
            pltpu.VMEM((ITERS, nz, 1, n), f32),
            pltpu.VMEM((1, n), f32),
            pltpu.VMEM((nb, rows, depth), f32),
            pltpu.VMEM((nb, rows, depth), bf16),
            pltpu.VMEM((nb, rows, depth), bf16),
            pltpu.VMEM((nv, st, patches * rows), bf16),
            pltpu.VMEM((nv, st, patches * rows), bf16),
            *sems,
        ],
        compiler_params=pltpu.CompilerParams(collective_id=0, has_side_effects=True),
        name="couple",
    )(latents, noise, offsets.reshape(rows, 4), times)
    width = embed.shape[1]
    tile = min(width, 1024)
    return pl.pallas_call(
        embed_tokens,
        grid=(width // tile,),
        out_shape=jax.ShapeDtypeStruct((rows, st, width), bf16),
        in_specs=[
            pl.BlockSpec(tokens.shape, lambda i: (0, 0, 0)),
            pl.BlockSpec((embed.shape[0], tile), lambda i: (0, i)),
        ],
        out_specs=pl.BlockSpec((rows, st, tile), lambda i: (0, 0, i)),
        scratch_shapes=[pltpu.VMEM((rows * st, embed.shape[0]), bf16)],
        name="embed",
    )(tokens, embed)


def solution(mesh):
    placed = (P("clip", "val"), P("clip", "val"), P("clip", None, None), P("clip"), P())
    return jax.shard_map(
        functools.partial(on_device, mesh.shape["clip"], mesh.shape["val"]),
        mesh=mesh,
        in_specs=placed,
        out_specs=P("clip", "val", None),
        check_vma=False,
    )
```

```python
import functools
import math

import jax
import jax.numpy as jnp
from jax import lax
from jax.experimental import pallas as pl
from jax.experimental.pallas import tpu as pltpu
from jax.sharding import PartitionSpec as P

P_SIZE = 64
FR = 2
GW = 16
GH = 4
ITERS = 4
STOP = 99
S = FR * GH * GW
LOG2E = 1.4426950408889634


def each(n, step):
    def body(i, carry):
        step(i)
        return carry

    lax.fori_loop(0, n, body, 0)


def far_first(n, i):
    return n // 2 + (2 * lax.rem(i, 2) - 1) * ((i + 1) // 2)


def turn(x, patches):
    return jnp.concatenate([x[:, p * S:(p + 1) * S] for p in range(patches)], axis=0).T


def couple(nz, nb, nv, lat, noise, off, times, out, pw, lg, part, rv, g, ex, urow, pb, rp, ms, la,
           w_s, w_r, l_s, l_r, r_s, r_r, g_s, g_r, e_s, e_r, c_s, c_r, a_s, a_r, p_s, p_r):
    nl, nx = nv // 2, nb // 2
    rows, depth = lat.shape
    patches = depth // S
    wide = nz * rows
    n = nb * wide
    st = S // nv
    width = patches * rows
    clip = lax.axis_index("clip")
    v = lax.axis_index("val")
    z, b = clip // nb, lax.rem(clip, nb)
    h, x = b // nx, lax.rem(b, nx)
    l, k = v // 2, lax.rem(v, 2)
    left = []

    def at(z_, b_, v_):
        return {"clip": z_ * nb + b_, "val": v_}

    def send(src, dst, s_sem, r_sem, where):
        return pltpu.make_async_remote_copy(src, dst, s_sem, r_sem, device_id=where)

    def launch(count, copy):
        each(count, lambda i: copy(i).start())
        left.append(lambda: each(count, lambda i: copy(i).wait_send()))

    def finish():
        for step in left:
            step()

    def halt(stage, value):
        if STOP != stage:
            return False
        out[...] = jnp.broadcast_to(jnp.sum(value), out.shape).astype(out.dtype)
        finish()
        return True

    def z_of(i):
        return lax.rem(z + far_first(nz, i), nz)

    def b_of(i):
        return jnp.where(i < nx, (1 - h) * nx + lax.rem(x + i, nx), h * nx + lax.rem(x + i + 1, nx))

    def v_of(i):
        return lax.rem(v + 1 + i, nv)

    barrier = pltpu.get_barrier_semaphore()
    each(nb - 1, lambda i: pl.semaphore_signal(barrier, inc=1, device_id=at(z, b_of(i), v)))
    each(nz - 1, lambda i: pl.semaphore_signal(barrier, inc=1, device_id=at(z_of(i), b, v)))
    each(nv - 1, lambda i: pl.semaphore_signal(barrier, inc=1, device_id=at(z, b, v_of(i))))

    rowi = lax.broadcasted_iota(jnp.int32, (rows, S), 0)
    lane = lax.broadcasted_iota(jnp.int32, (rows, S), 1)
    first = lane < GH * GW
    sy = jnp.zeros((rows, S), jnp.int32)
    sx = jnp.zeros((rows, S), jnp.int32)
    for i in range(rows):
        here = rowi == i
        sy = jnp.where(here, jnp.where(first, off[0, i], off[2, i]), sy)
        sx = jnp.where(here, jnp.where(first, off[1, i], off[3, i]), sx)
    col = lane & (GW - 1)
    row = (lane // GW) & (GH - 1)
    for p in range(patches):
        t = noise[:, p * S:(p + 1) * S].astype(jnp.float32)
        for bit in (1, 2, 4, 8):
            turned = jnp.where(col >= bit, pltpu.roll(t, bit, 1), pltpu.roll(t, S - GW + bit, 1))
            t = jnp.where((sx & bit) != 0, turned, t)
        for bit in (1, 2):
            turned = jnp.where(
                row >= bit, pltpu.roll(t, bit * GW, 1), pltpu.roll(t, S - GH * GW + bit * GW, 1)
            )
            t = jnp.where((sy & bit) != 0, turned, t)
        pw[h, k, z, :, p * S:(p + 1) * S] = t.astype(jnp.bfloat16)
    lg[b] = lat[...]
    pl.semaphore_wait(barrier, (nz - 1) + (nb - 1) + (nv - 1))
    if halt(0, sx.astype(jnp.float32)):
        return

    launch(nb - 1, lambda i: send(lat, lg.at[b], l_s.at[i], l_r.at[b], at(z, b_of(i), v)))
    mine = pw.at[h, k, z]
    launch(nz - 1, lambda i: send(mine, mine, w_s.at[i], w_r.at[z], at(z_of(i), b, v)))

    ms[...] = turn(lat[...].astype(jnp.float32), patches).astype(jnp.bfloat16).reshape(nv, st, width)
    launch(nv - 1, lambda i: send(ms.at[v_of(i)], la.at[v], a_s.at[i], a_r.at[v], at(z, b, v_of(i))))
    la[v] = ms[v]

    def w_wait(i):
        here = pw.at[h, k, z_of(i)]
        send(here, here, w_s.at[i], w_r.at[z_of(i)], at(z_of(i), b, v)).wait_recv()

    def l_wait(i):
        bt = b_of(i)
        send(lat, lg.at[bt], l_s.at[i], l_r.at[bt], at(z, bt, v)).wait_recv()

    each(nz - 1, w_wait)
    neighbour = at(z, b, l * 2 + (1 - k))
    facing = at(z, (1 - h) * nx + x, v)
    panel = pw.at[h, k]
    launch(1, lambda i: send(panel, panel, p_s.at[0], p_r.at[0], neighbour))
    noises = pw[h, k].reshape(wide, depth)
    square = noises.astype(jnp.float32)
    square = jnp.sum(square * square, axis=1, keepdims=True)
    diagonal = lax.broadcasted_iota(jnp.int32, (wide, wide), 0) == lax.broadcasted_iota(
        jnp.int32, (wide, wide), 1
    )
    square = jnp.sum(jnp.where(diagonal, square, 0.0), axis=0, keepdims=True)

    def block(half):
        gram = lax.dot_general(
            lg[pl.ds(half * nx, nx)].reshape(nx * rows, depth),
            pw[h, k].reshape(wide, depth),
            (((1,), (1,)), ((), ())),
            preferred_element_type=jnp.float32,
        )
        part[pl.ds(half * nx, nx)] = (square - 2.0 * gram).reshape(nx, rows, wide)

    def r_copy(vt):
        return send(part.at[vt], rv.at[v], r_s.at[vt], r_r.at[v], at(z, b, vt))

    def r_send(half):
        def one(i):
            vt = half * nx + lax.rem(x + i, nx)

            @pl.when(vt != v)
            def _():
                r_copy(vt).start()

        each(nx, one)

    each(nx - 1, lambda i: l_wait(nx + i))
    block(h)
    r_send(h)
    each(nx, l_wait)
    block(1 - h)
    r_send(1 - h)
    left.append(lambda: each(nv - 1, lambda i: r_copy(v_of(i)).wait_send()))
    rv[v] = part[v]
    if halt(1, part[0]):
        return

    def r_wait(i):
        vt = v_of(i)
        send(part.at[vt], rv.at[vt], r_s.at[vt], r_r.at[vt], at(z, b, vt)).wait_recv()

    each(nv - 1, r_wait)
    volume = float(nv * depth)
    entropy = 0.5 / math.sqrt(volume)

    def columns(b_):
        return pl.ds(pl.multiple_of(b_ * wide, wide), wide)

    g[l, :, columns(b)] = jnp.sum(rv[...], axis=0) * (LOG2E / (volume * entropy))
    if halt(2, g[l, :, columns(b)]):
        return

    n_plane = nl * nb
    own = l * nb + b

    def g_of(i):
        return lax.rem(own + 1 + i, n_plane)

    def g_at(q):
        return at(z, lax.rem(q, nb), (q // nb) * 2 + k)

    source = g.at[l, :, columns(b)]
    launch(n_plane - 1, lambda i: send(source, source, g_s.at[i], g_r.at[own], g_at(g_of(i))))

    def g_wait(i):
        q = g_of(i)
        here = g.at[q // nb, :, columns(lax.rem(q, nb))]
        send(here, here, g_s.at[i], g_r.at[q], g_at(q)).wait_recv()

    each(n_plane - 1, g_wait)
    launch(1, lambda i: send(panel, panel, p_s.at[1], p_r.at[1], facing))
    if halt(3, g[...]):
        return

    blocks = n // S
    height = nl * rows
    n_ring = 2 * nz
    own_e = z * 2 + k

    def tile(c, first=0, count=nl):
        return g[pl.ds(first, count), :, c * S:(c + 1) * S].reshape(count * rows, S)

    def row_stats(dual, first=0, count=nl):
        top = dual[0:1] - tile(0, first, count)
        for c in range(1, blocks):
            top = jnp.maximum(top, dual[c:c + 1] - tile(c, first, count))
        top = jnp.max(top, axis=1, keepdims=True)
        total = jnp.exp2(dual[0:1] - tile(0, first, count) - top)
        for c in range(1, blocks):
            total = total + jnp.exp2(dual[c:c + 1] - tile(c, first, count) - top)
        return top, jnp.sum(total, axis=1, keepdims=True)

    def e_of(i):
        return lax.rem(own_e + far_first(n_ring, i), n_ring)

    def e_at(q):
        return at(q // 2, b, l * 2 + lax.rem(q, 2))

    dual = jnp.zeros((blocks, S), jnp.float32)
    for it in range(ITERS):
        top, total = row_stats(dual)
        row_dual = -(top + jnp.log2(total))
        for c in range(blocks):
            t = row_dual - tile(c)
            top = jnp.max(t, axis=0, keepdims=True)
            total = jnp.sum(jnp.exp2(t - top), axis=0, keepdims=True)
            ex[it, own_e, c:c + 1] = top + jnp.log2(total)
        here = ex.at[it, own_e]

        def e_copy(i, it=it, here=here):
            return send(here, here, e_s.at[it, i], e_r.at[it, own_e], e_at(e_of(i)))

        def e_wait(i, it=it):
            q = e_of(i)
            there = ex.at[it, q]
            send(there, there, e_s.at[it, i], e_r.at[it, q], e_at(q)).wait_recv()

        launch(n_ring - 1, e_copy)
        if it == ITERS - 1:
            passed = pw.at[1 - h, k]
            send(passed, passed, p_s.at[1], p_r.at[1], facing).wait_recv()
            launch(1, lambda i: send(passed, passed, p_s.at[2], p_r.at[2], neighbour))
        each(n_ring - 1, e_wait)
        parts = ex[it]
        top = jnp.max(parts, axis=0)
        total = jnp.sum(jnp.exp2(parts - top[None]), axis=0)
        dual = -(top + jnp.log2(total))
        if halt(4 + it, dual):
            return

    for c in range(blocks):
        urow[:, c * S:(c + 1) * S] = dual[c:c + 1]
    count = nl // 2
    start = h * count
    top, total = row_stats(dual, start, count)
    weights = []
    for half in range(2):
        here = columns(half * nx + x)
        t = urow[:, here] - g[pl.ds(start, count), :, here].reshape(count * rows, wide)
        weights.append((jnp.exp2(t - top) / total).astype(jnp.bfloat16))

    there = pw.at[h, 1 - k]
    send(there, there, p_s.at[0], p_r.at[0], neighbour).wait_recv()
    there = pw.at[1 - h, 1 - k]
    send(there, there, p_s.at[2], p_r.at[2], neighbour).wait_recv()
    for kk in range(2):
        coupled = jnp.dot(weights[0], pw[0, kk].reshape(wide, depth), preferred_element_type=jnp.float32)
        coupled += jnp.dot(weights[1], pw[1, kk].reshape(wide, depth), preferred_element_type=jnp.float32)
        for i in range(count):
            piece = turn(coupled[i * rows:(i + 1) * rows], patches).astype(jnp.bfloat16)
            pb[i, :, kk] = piece.reshape(nv, st, width)
    if halt(8, pb[0, 0, 0].astype(jnp.float32)):
        return

    def c_copy(i, vt):
        return send(pb.at[i, vt], rp.at[x, l], c_s.at[i * nv + vt], c_r.at[x * nl + l], at(z, h * nx + 2 * i + k, vt))

    def c_each(act):
        def one(j):
            i, vt = j // nv, lax.rem(v + j, nv)

            @pl.when((2 * i + k != x) | (vt != v))
            def _():
                act(i, vt)

        each(count * nv, one)

    c_each(lambda i, vt: c_copy(i, vt).start())
    left.append(lambda: c_each(lambda i, vt: c_copy(i, vt).wait_send()))
    parity = lax.rem(x, 2)

    @pl.when(parity == k)
    def _():
        rp[x, l] = pb[x // 2, v]

    def c_wait(q):
        xt, lt = q // nl, lax.rem(q, nl)
        vt = lt * 2 + parity

        @pl.when((xt != x) | (vt != v))
        def _():
            send(pb.at[0, 0], rp.at[xt, lt], c_s.at[0], c_r.at[q], at(z, h * nx + xt, vt)).wait_recv()

    def a_wait(i):
        vt = v_of(i)
        send(ms.at[vt], la.at[vt], a_s.at[i], a_r.at[vt], at(z, b, vt)).wait_recv()

    lane = lax.broadcasted_iota(jnp.int32, (st, width), 1) & (rows - 1)
    time = jnp.zeros((st, width), jnp.float32)
    for i in range(rows):
        time = jnp.where(lane == i, times[i], time)
    clip_of = lax.broadcasted_iota(jnp.int32, (rows, st, width), 0)
    keep = (lax.broadcasted_iota(jnp.int32, (rows, st, width), 2) & (rows - 1)) == clip_of
    from_lane = lax.broadcasted_iota(jnp.int32, (width, nv * patches), 0) // rows
    to_patch = lax.broadcasted_iota(jnp.int32, (width, nv * patches), 1)
    each(nv - 1, a_wait)
    each(nx * nl, c_wait)
    made = jnp.zeros((rows * st, nv * patches), jnp.float32)
    for j in range(nv):
        coupled = rp[0, j // 2, j % 2].astype(jnp.float32)
        for xt in range(1, nx):
            coupled = coupled + rp[xt, j // 2, j % 2].astype(jnp.float32)
        mixed = (1.0 - time) * la[j].astype(jnp.float32) + time * coupled
        spread = jnp.where(keep, mixed[None], 0.0).reshape(rows * st, width).astype(jnp.bfloat16)
        pick = jnp.where(to_patch == from_lane + j * patches, 1.0, 0.0).astype(jnp.bfloat16)
        made = made + jnp.dot(spread, pick, preferred_element_type=jnp.float32)
    out[...] = made.astype(jnp.bfloat16)

    finish()


def on_device(nc, nv, latents, noise, offsets, times, embed):
    nb = nv
    nz, nl, nx = nc // nb, nv // 2, nb // 2
    rows, depth = latents.shape
    patches = depth // S
    st = S // nv
    wide = nz * rows
    n = nc * rows
    width = patches * rows
    f32, bf16 = jnp.float32, jnp.bfloat16
    dma = pltpu.SemaphoreType.DMA
    vmem = pl.BlockSpec(memory_space=pltpu.VMEM)
    smem = pl.BlockSpec(memory_space=pltpu.SMEM)
    sems = []
    for sent, got in (
        (nz, nz), (nb, nb), (nv, nv), (nl * nb, nl * nb), ((ITERS, 2 * nz),) * 2, (nl // 2 * nv, nx * nl), (nv, nv), (3, 3)
    ):
        sems += [dma(c if isinstance(c, tuple) else (c,)) for c in (sent, got)]
    tokens = pl.pallas_call(
        functools.partial(couple, nz, nb, nv),
        out_shape=jax.ShapeDtypeStruct((rows * st, nv * patches), bf16),
        in_specs=[vmem, vmem, smem, smem],
        out_specs=vmem,
        scratch_shapes=[
            pltpu.VMEM((2, 2, nz, rows, depth), bf16),
            pltpu.VMEM((nb, rows, depth), bf16),
            pltpu.VMEM((nb, rows, wide), f32),
            pltpu.VMEM((nv, rows, wide), f32),
            pltpu.VMEM((nl, rows, n), f32),
            pltpu.VMEM((ITERS, 2 * nz, n // S, S), f32),
            pltpu.VMEM((1, n), f32),
            pltpu.VMEM((nl // 2, nv, 2, st, width), bf16),
            pltpu.VMEM((nx, nl, 2, st, width), bf16),
            pltpu.VMEM((nv, st, width), bf16),
            pltpu.VMEM((nv, st, width), bf16),
            *sems,
        ],
        compiler_params=pltpu.CompilerParams(collective_id=0, has_side_effects=True),
        name="couple",
    )(latents, noise, offsets.reshape(rows, 4).T, times)
    made = jnp.dot(tokens, embed, preferred_element_type=f32).astype(bf16)
    return made.reshape(rows, st, embed.shape[1])


def solution(mesh):
    placed = (P("clip", "val"), P("clip", "val"), P("clip", None, None), P("clip"), P())
    return jax.shard_map(
        functools.partial(on_device, mesh.shape["clip"], mesh.shape["val"]),
        mesh=mesh,
        in_specs=placed,
        out_specs=P("clip", "val", None),
        check_vma=False,
    )
```

```python
import functools
import math

import jax
import jax.numpy as jnp
from jax import lax
from jax.experimental import pallas as pl
from jax.experimental.pallas import tpu as pltpu
from jax.sharding import PartitionSpec as P

P_SIZE = 64
FR = 2
GW = 16
GH = 4
ITERS = 4
S = FR * GH * GW
LOG2E = 1.4426950408889634


def ring(n):
    return sorted(range(1, n), key=lambda i: -min(i, n - i))


def turn(x, patches):
    return jnp.concatenate([x[:, p * S:(p + 1) * S] for p in range(patches)], axis=0).T


def couple(nz, nb, nv, lat, noise, off, times, out, pw, lg, part, rv, g, ex, urow, pb, rp, ms, la,
           w_s, w_r, l_s, l_near, l_far, r_s, r_r, g_s, g_r, e_s, e_r, c_s, c_r, a_s, a_r, p_s, p_r):
    nl, nx = nv // 2, nb // 2
    rows, depth = lat.shape
    patches = depth // S
    wide = nz * rows
    n = nb * wide
    st = S // nv
    width = patches * rows
    clip = lax.axis_index("clip")
    v = lax.axis_index("val")
    z, b = clip // nb, lax.rem(clip, nb)
    h, x = b // nx, lax.rem(b, nx)
    l, k = v // 2, lax.rem(v, 2)
    y = h * nl + l
    left = []

    def at(z_, b_, v_):
        return {"clip": z_ * nb + b_, "val": v_}

    def send(src, dst, s_sem, r_sem, where):
        pltpu.make_async_remote_copy(src, dst, s_sem, r_sem, device_id=where).start()

    def came(like, sem):
        pltpu.make_async_remote_copy(like, like, sem, sem, device_id=at(z, b, v)).wait_recv()

    def gone(like, sem):
        left.append(lambda: pltpu.make_async_remote_copy(like, like, sem, sem, device_id=at(z, b, v)).wait_send())

    def finish():
        while left:
            left.pop()()

    z_peers = [lax.rem(z + i, nz) for i in ring(nz)]
    far_peers = [(1 - h) * nx + lax.rem(x + i, nx) for i in ring(nx) + [0]]
    near_peers = [h * nx + lax.rem(x + i, nx) for i in ring(nx)]
    v_peers = [lax.rem(v + i, nv) for i in range(1, nv)]

    barrier = pltpu.get_barrier_semaphore()
    for bt in far_peers + near_peers:
        pl.semaphore_signal(barrier, inc=1, device_id=at(z, bt, v))
    for zt in z_peers:
        pl.semaphore_signal(barrier, inc=1, device_id=at(zt, b, v))
    for vt in v_peers:
        pl.semaphore_signal(barrier, inc=1, device_id=at(z, b, vt))

    rowi = lax.broadcasted_iota(jnp.int32, (rows, S), 0)
    lane = lax.broadcasted_iota(jnp.int32, (rows, S), 1)
    first = lane < GH * GW
    sy = jnp.zeros((rows, S), jnp.int32)
    sx = jnp.zeros((rows, S), jnp.int32)
    for i in range(rows):
        here = rowi == i
        sy = jnp.where(here, jnp.where(first, off[0, i], off[2, i]), sy)
        sx = jnp.where(here, jnp.where(first, off[1, i], off[3, i]), sx)
    col = lane & (GW - 1)
    row = (lane // GW) & (GH - 1)
    for p in range(patches):
        t = noise[:, p * S:(p + 1) * S].astype(jnp.float32)
        for bit in (1, 2, 4, 8):
            turned = jnp.where(col >= bit, pltpu.roll(t, bit, 1), pltpu.roll(t, S - GW + bit, 1))
            t = jnp.where((sx & bit) != 0, turned, t)
        for bit in (1, 2):
            turned = jnp.where(
                row >= bit, pltpu.roll(t, bit * GW, 1), pltpu.roll(t, S - GH * GW + bit * GW, 1)
            )
            t = jnp.where((sy & bit) != 0, turned, t)
        pw[h, k, z, :, p * S:(p + 1) * S] = t.astype(jnp.bfloat16)
    lg[b] = lat[...]
    pl.semaphore_wait(barrier, (nz - 1) + (nb - 1) + (nv - 1))

    for bt in far_peers:
        send(lat, lg.at[b], l_s, l_far, at(z, bt, v))
    for bt in near_peers:
        send(lat, lg.at[b], l_s, l_near, at(z, bt, v))
    gone(lg.at[pl.ds(0, nb - 1)], l_s)
    mine = pw.at[h, k, z]
    for zt in z_peers:
        send(mine, mine, w_s, w_r, at(zt, b, v))
    if nz > 1:
        gone(pw.at[h, k, pl.ds(0, nz - 1)], w_s)

    ms[...] = turn(lat[...].astype(jnp.float32), patches).astype(jnp.bfloat16).reshape(nv, st, width)
    for vt in v_peers:
        send(ms.at[vt], la.at[v], a_s, a_r, at(z, b, vt))
    gone(ms.at[pl.ds(0, nv - 1)], a_s)
    la[v] = ms[v]

    if nz > 1:
        came(pw.at[h, k, pl.ds(0, nz - 1)], w_r)
    neighbour = at(z, b, l * 2 + (1 - k))
    facing = at(z, (1 - h) * nx + x, v)
    panel = pw.at[h, k]
    send(panel, panel, p_s.at[0], p_r.at[0], neighbour)
    gone(panel, p_s.at[0])
    noises = pw[h, k].reshape(wide, depth)
    square = noises.astype(jnp.float32)
    square = jnp.sum(square * square, axis=1, keepdims=True)
    diagonal = lax.broadcasted_iota(jnp.int32, (wide, wide), 0) == lax.broadcasted_iota(
        jnp.int32, (wide, wide), 1
    )
    square = jnp.sum(jnp.where(diagonal, square, 0.0), axis=0, keepdims=True)

    def block(half):
        gram = lax.dot_general(
            lg[pl.ds(half * nx, nx)].reshape(nx * rows, depth),
            pw[h, k].reshape(wide, depth),
            (((1,), (1,)), ((), ())),
            preferred_element_type=jnp.float32,
        )
        part[pl.ds(half * nx, nx)] = (square - 2.0 * gram).reshape(nx, rows, wide)

    def r_send(half):
        for i in range(nx):
            vt = half * nx + lax.rem(x + i, nx)

            @pl.when(vt != v)
            def _():
                send(part.at[vt], rv.at[v], r_s, r_r, at(z, b, vt))

    came(lg.at[pl.ds(0, nx - 1)], l_near)
    block(h)
    r_send(h)
    came(lg.at[pl.ds(0, nx)], l_far)
    block(1 - h)
    r_send(1 - h)
    gone(part.at[pl.ds(0, nv - 1)], r_s)
    rv[v] = part[v]
    came(rv.at[pl.ds(0, nv - 1)], r_r)
    volume = float(nv * depth)
    entropy = 0.5 / math.sqrt(volume)

    piece = g.at[b * nl + l]
    piece[...] = jnp.sum(rv[...], axis=0) * (LOG2E / (volume * entropy))

    ny = 2 * nl
    steps = [(i, j) for i in range(ny) for j in range(nx) if i or j]
    for i, j in sorted(steps, key=lambda s: -min(s[0], ny - s[0]) - min(s[1], nx - s[1])):
        yt, xt = lax.rem(y + i, ny), lax.rem(x + j, nx)
        send(piece, piece, g_s, g_r, at(z, yt // nl * nx + xt, lax.rem(yt, nl) * 2 + k))
    pieces = g.at[pl.ds(0, nl * nb - 1)]
    gone(pieces, g_s)
    came(pieces, g_r)
    send(panel, panel, p_s.at[1], p_r.at[1], facing)
    gone(panel, p_s.at[1])

    blocks = nb
    own_e = z * 2 + k

    def tile(c, first=0, count=nl):
        return g[pl.ds(c * nl + first, count)].reshape(count * rows, wide)

    def row_stats(dual, first=0, count=nl):
        top = dual[0:1] - tile(0, first, count)
        for c in range(1, blocks):
            top = jnp.maximum(top, dual[c:c + 1] - tile(c, first, count))
        top = jnp.max(top, axis=1, keepdims=True)
        total = jnp.exp2(dual[0:1] - tile(0, first, count) - top)
        for c in range(1, blocks):
            total = total + jnp.exp2(dual[c:c + 1] - tile(c, first, count) - top)
        return top, jnp.sum(total, axis=1, keepdims=True)

    e_peers = [(z_, q) for z_ in z_peers for q in (1 - k, k)] + [(z, 1 - k)]

    dual = jnp.zeros((blocks, wide), jnp.float32)
    for it in range(ITERS):
        top, total = row_stats(dual)
        row_dual = -(top + jnp.log2(total))
        for c in range(blocks):
            t = row_dual - tile(c)
            top = jnp.max(t, axis=0, keepdims=True)
            total = jnp.sum(jnp.exp2(t - top), axis=0, keepdims=True)
            ex[it, own_e, c:c + 1] = top + jnp.log2(total)
        here = ex.at[it, own_e]

        for zt, kt in e_peers:
            send(here, here, e_s.at[it], e_r.at[it], at(zt, b, l * 2 + kt))
        others = ex.at[it, pl.ds(0, 2 * nz - 1)]
        gone(others, e_s.at[it])
        if it == ITERS - 1:
            passed = pw.at[1 - h, k]
            came(passed, p_r.at[1])
            send(passed, passed, p_s.at[2], p_r.at[2], neighbour)
            gone(passed, p_s.at[2])
        came(others, e_r.at[it])
        parts = ex[it]
        top = jnp.max(parts, axis=0)
        total = jnp.sum(jnp.exp2(parts - top[None]), axis=0)
        dual = -(top + jnp.log2(total))

    urow[...] = dual
    count = nl // 2
    start = h * count
    top, total = row_stats(dual, start, count)
    weights = []
    for half in range(2):
        at_x = half * nx + x
        t = urow[pl.ds(at_x, 1)] - g[pl.ds(at_x * nl + start, count)].reshape(count * rows, wide)
        weights.append((jnp.exp2(t - top) / total).astype(jnp.bfloat16))

    came(pw.at[h, 1 - k], p_r.at[0])
    came(pw.at[1 - h, 1 - k], p_r.at[2])
    for kk in range(2):
        coupled = jnp.dot(weights[0], pw[0, kk].reshape(wide, depth), preferred_element_type=jnp.float32)
        coupled += jnp.dot(weights[1], pw[1, kk].reshape(wide, depth), preferred_element_type=jnp.float32)
        for i in range(count):
            piece = turn(coupled[i * rows:(i + 1) * rows], patches).astype(jnp.bfloat16)
            pb[i * nv:(i + 1) * nv, kk] = piece.reshape(nv, st, width)

    parity = lax.rem(x, 2)
    slot = x * nl + l
    for vt in v_peers + [v]:
        for i in range(count):
            src, dst, xt = pb.at[i * nv + vt], rp.at[slot], 2 * i + k
            if vt is not v:
                send(src, dst, c_s, c_r, at(z, h * nx + xt, vt))
            else:

                @pl.when(xt != x)
                def _():
                    send(src, dst, c_s, c_r, at(z, h * nx + xt, vt))

    @pl.when(parity == k)
    def _():
        rp[slot] = pb[x // 2 * nv + v]

    finish()
    lane = lax.broadcasted_iota(jnp.int32, (st, width), 1) & (rows - 1)
    time = jnp.zeros((st, width), jnp.float32)
    for i in range(rows):
        time = jnp.where(lane == i, times[i], time)
    clip_of = lax.broadcasted_iota(jnp.int32, (rows, st, width), 0)
    keep = (lax.broadcasted_iota(jnp.int32, (rows, st, width), 2) & (rows - 1)) == clip_of
    from_lane = lax.broadcasted_iota(jnp.int32, (width, nv * patches), 0) // rows
    to_patch = lax.broadcasted_iota(jnp.int32, (width, nv * patches), 1)
    came(la.at[pl.ds(0, nv - 1)], a_r)
    number = nx * nl

    @pl.when(parity == k)
    def _():
        came(rp.at[pl.ds(0, number - 1)], c_r)

    @pl.when(parity != k)
    def _():
        came(rp, c_r)

    made = jnp.zeros((rows * st, nv * patches), jnp.float32)
    for j in range(nv):
        coupled = rp[j // 2, j % 2].astype(jnp.float32)
        for xt in range(1, nx):
            coupled = coupled + rp[xt * nl + j // 2, j % 2].astype(jnp.float32)
        mixed = (1.0 - time) * la[j].astype(jnp.float32) + time * coupled
        spread = jnp.where(keep, mixed[None], 0.0).reshape(rows * st, width).astype(jnp.bfloat16)
        pick = jnp.where(to_patch == from_lane + j * patches, 1.0, 0.0).astype(jnp.bfloat16)
        made = made + jnp.dot(spread, pick, preferred_element_type=jnp.float32)
    out[...] = made.astype(jnp.bfloat16)

    @pl.when(parity == k)
    def _():
        gone(pb.at[pl.ds(0, number - 1)], c_s)
        finish()

    @pl.when(parity != k)
    def _():
        gone(pb, c_s)
        finish()


def on_device(nc, nv, latents, noise, offsets, times, embed):
    nb = nv
    nz, nl, nx = nc // nb, nv // 2, nb // 2
    rows, depth = latents.shape
    patches = depth // S
    st = S // nv
    wide = nz * rows
    width = patches * rows
    f32, bf16 = jnp.float32, jnp.bfloat16
    vmem = pl.BlockSpec(memory_space=pltpu.VMEM)
    smem = pl.BlockSpec(memory_space=pltpu.SMEM)
    sems = []
    for shape in (1, 1, 1, 1, 1, 1, 1, 1, 1, ITERS, ITERS, 1, 1, 1, 1, 3, 3):
        sems.append(pltpu.SemaphoreType.DMA if shape == 1 else pltpu.SemaphoreType.DMA((shape,)))
    tokens = pl.pallas_call(
        functools.partial(couple, nz, nb, nv),
        out_shape=jax.ShapeDtypeStruct((rows * st, nv * patches), bf16),
        in_specs=[vmem, vmem, smem, smem],
        out_specs=vmem,
        scratch_shapes=[
            pltpu.VMEM((2, 2, nz, rows, depth), bf16),
            pltpu.VMEM((nb, rows, depth), bf16),
            pltpu.VMEM((nb, rows, wide), f32),
            pltpu.VMEM((nv, rows, wide), f32),
            pltpu.VMEM((nb * nl, rows, wide), f32),
            pltpu.VMEM((ITERS, 2 * nz, nb, wide), f32),
            pltpu.VMEM((nb, wide), f32),
            pltpu.VMEM((nl // 2 * nv, 2, st, width), bf16),
            pltpu.VMEM((nx * nl, 2, st, width), bf16),
            pltpu.VMEM((nv, st, width), bf16),
            pltpu.VMEM((nv, st, width), bf16),
            *sems,
        ],
        compiler_params=pltpu.CompilerParams(collective_id=0, has_side_effects=True),
        name="couple",
    )(latents, noise, offsets.reshape(rows, 4).T, times)
    made = jnp.dot(tokens, embed, preferred_element_type=f32).astype(bf16)
    return made.reshape(rows, st, embed.shape[1])


def solution(mesh):
    placed = (P("clip", "val"), P("clip", "val"), P("clip", None, None), P("clip"), P())
    return jax.shard_map(
        functools.partial(on_device, mesh.shape["clip"], mesh.shape["val"]),
        mesh=mesh,
        in_specs=placed,
        out_specs=P("clip", "val", None),
        check_vma=False,
    )
```

```python
import functools
import math

import jax
import jax.numpy as jnp
from jax import lax
from jax.experimental import pallas as pl
from jax.experimental.pallas import tpu as pltpu
from jax.sharding import PartitionSpec as P

P_SIZE = 64
FR = 2
GW = 16
GH = 4
ITERS = 4
VMEM = 16 << 20
S = FR * GH * GW
LOG2E = 1.4426950408889634


def ring(n):
    return sorted(range(1, n), key=lambda i: -min(i, n - i))


def turn(x, patches):
    return jnp.concatenate([x[:, p * S:(p + 1) * S] for p in range(patches)], axis=0).T


def couple(nz, nb, nv, lat_in, noise_in, off_in, times_in, out, lat, noise, off, times, pw, lg, part, rv, g, ex, urow, pb, rp, ms, la,
           w_s, w_r, l_s, l_near, l_far, r_s, r_r, g_s, g_r, e_s, e_r, c_s, c_r, a_s, a_r, p_s, p_r, i_s):
    nl, nx = nv // 2, nb // 2
    rows, depth = lat.shape
    patches = depth // S
    wide = nz * rows
    n = nb * wide
    st = S // nv
    width = patches * rows
    clip = lax.axis_index("clip")
    v = lax.axis_index("val")
    z, b = clip // nb, lax.rem(clip, nb)
    h, x = b // nx, lax.rem(b, nx)
    l, k = v // 2, lax.rem(v, 2)
    y = h * nl + l
    left = []

    def at(z_, b_, v_):
        return {"clip": z_ * nb + b_, "val": v_}

    def send(src, dst, s_sem, r_sem, where):
        pltpu.make_async_remote_copy(src, dst, s_sem, r_sem, device_id=where).start()

    def came(like, sem):
        pltpu.make_async_remote_copy(like, like, sem, sem, device_id=at(z, b, v)).wait_recv()

    def gone(like, sem):
        left.append(lambda: pltpu.make_async_remote_copy(like, like, sem, sem, device_id=at(z, b, v)).wait_send())

    def finish():
        while left:
            left.pop()()

    z_peers = [lax.rem(z + i, nz) for i in ring(nz)]
    far_peers = [(1 - h) * nx + lax.rem(x + i, nx) for i in ring(nx) + [0]]
    near_peers = [h * nx + lax.rem(x + i, nx) for i in ring(nx)]
    v_peers = [lax.rem(v + i, nv) for i in range(1, nv)]

    barrier = pltpu.get_barrier_semaphore()
    for bt in far_peers + near_peers:
        pl.semaphore_signal(barrier, inc=1, device_id=at(z, bt, v))
    for zt in z_peers:
        pl.semaphore_signal(barrier, inc=1, device_id=at(zt, b, v))
    for vt in v_peers:
        pl.semaphore_signal(barrier, inc=1, device_id=at(z, b, vt))

    loads = [
        pltpu.make_async_copy(src, dst, i_s.at[i])
        for i, (src, dst) in enumerate(((off_in, off), (noise_in, noise), (lat_in, lat), (times_in, times)))
    ]
    for load in loads:
        load.start()

    rowi = lax.broadcasted_iota(jnp.int32, (rows, S), 0)
    lane = lax.broadcasted_iota(jnp.int32, (rows, S), 1)
    first = lane < GH * GW
    sy = jnp.zeros((rows, S), jnp.int32)
    sx = jnp.zeros((rows, S), jnp.int32)
    loads[0].wait()
    for i in range(rows):
        here = rowi == i
        sy = jnp.where(here, jnp.where(first, off[0, i], off[2, i]), sy)
        sx = jnp.where(here, jnp.where(first, off[1, i], off[3, i]), sx)
    col = lane & (GW - 1)
    row = (lane // GW) & (GH - 1)
    loads[1].wait()
    for p in range(patches):
        t = noise[:, p * S:(p + 1) * S].astype(jnp.float32)
        for bit in (1, 2, 4, 8):
            turned = jnp.where(col >= bit, pltpu.roll(t, bit, 1), pltpu.roll(t, S - GW + bit, 1))
            t = jnp.where((sx & bit) != 0, turned, t)
        for bit in (1, 2):
            turned = jnp.where(
                row >= bit, pltpu.roll(t, bit * GW, 1), pltpu.roll(t, S - GH * GW + bit * GW, 1)
            )
            t = jnp.where((sy & bit) != 0, turned, t)
        pw[h, k, z, :, p * S:(p + 1) * S] = t.astype(jnp.bfloat16)
    loads[2].wait()
    loads[3].wait()
    lg[b] = lat[...]
    pl.semaphore_wait(barrier, (nz - 1) + (nb - 1) + (nv - 1))

    for bt in far_peers:
        send(lat, lg.at[b], l_s, l_far, at(z, bt, v))
    for bt in near_peers:
        send(lat, lg.at[b], l_s, l_near, at(z, bt, v))
    gone(lg.at[pl.ds(0, nb - 1)], l_s)
    mine = pw.at[h, k, z]
    for zt in z_peers:
        send(mine, mine, w_s, w_r, at(zt, b, v))
    if nz > 1:
        gone(pw.at[h, k, pl.ds(0, nz - 1)], w_s)

    ms[...] = turn(lat[...].astype(jnp.float32), patches).astype(jnp.bfloat16).reshape(nv, st, width)
    for vt in v_peers:
        send(ms.at[vt], la.at[v], a_s, a_r, at(z, b, vt))
    gone(ms.at[pl.ds(0, nv - 1)], a_s)
    la[v] = ms[v]

    if nz > 1:
        came(pw.at[h, k, pl.ds(0, nz - 1)], w_r)
    neighbour = at(z, b, l * 2 + (1 - k))
    facing = at(z, (1 - h) * nx + x, v)
    panel = pw.at[h, k]
    send(panel, panel, p_s.at[0], p_r.at[0], neighbour)
    gone(panel, p_s.at[0])
    noises = pw[h, k].reshape(wide, depth)
    square = noises.astype(jnp.float32)
    square = jnp.sum(square * square, axis=1, keepdims=True)
    diagonal = lax.broadcasted_iota(jnp.int32, (wide, wide), 0) == lax.broadcasted_iota(
        jnp.int32, (wide, wide), 1
    )
    square = jnp.sum(jnp.where(diagonal, square, 0.0), axis=0, keepdims=True)

    def block(half):
        gram = lax.dot_general(
            lg[pl.ds(half * nx, nx)].reshape(nx * rows, depth),
            pw[h, k].reshape(wide, depth),
            (((1,), (1,)), ((), ())),
            preferred_element_type=jnp.float32,
        )
        part[pl.ds(half * nx, nx)] = (square - 2.0 * gram).reshape(nx, rows, wide)

    def r_send(half):
        for i in range(nx):
            vt = half * nx + lax.rem(x + i, nx)

            @pl.when(vt != v)
            def _():
                send(part.at[vt], rv.at[v], r_s, r_r, at(z, b, vt))

    came(lg.at[pl.ds(0, nx - 1)], l_near)
    block(h)
    r_send(h)
    came(lg.at[pl.ds(0, nx)], l_far)
    block(1 - h)
    r_send(1 - h)
    gone(part.at[pl.ds(0, nv - 1)], r_s)
    rv[v] = part[v]
    came(rv.at[pl.ds(0, nv - 1)], r_r)
    volume = float(nv * depth)
    entropy = 0.5 / math.sqrt(volume)

    piece = g.at[b * nl + l]
    piece[...] = jnp.sum(rv[...], axis=0) * (LOG2E / (volume * entropy))

    ny = 2 * nl
    steps = [(i, j) for i in range(ny) for j in range(nx) if i or j]
    for i, j in sorted(steps, key=lambda s: -min(s[0], ny - s[0]) - min(s[1], nx - s[1])):
        yt, xt = lax.rem(y + i, ny), lax.rem(x + j, nx)
        send(piece, piece, g_s, g_r, at(z, yt // nl * nx + xt, lax.rem(yt, nl) * 2 + k))
    pieces = g.at[pl.ds(0, nl * nb - 1)]
    gone(pieces, g_s)
    came(pieces, g_r)
    send(panel, panel, p_s.at[1], p_r.at[1], facing)
    gone(panel, p_s.at[1])

    blocks = nb
    own_e = z * 2 + k

    def tile(c, first=0, count=nl):
        return g[pl.ds(c * nl + first, count)].reshape(count * rows, wide)

    def row_stats(dual, first=0, count=nl):
        top = dual[0:1] - tile(0, first, count)
        for c in range(1, blocks):
            top = jnp.maximum(top, dual[c:c + 1] - tile(c, first, count))
        top = jnp.max(top, axis=1, keepdims=True)
        total = jnp.exp2(dual[0:1] - tile(0, first, count) - top)
        for c in range(1, blocks):
            total = total + jnp.exp2(dual[c:c + 1] - tile(c, first, count) - top)
        return top, jnp.sum(total, axis=1, keepdims=True)

    e_peers = [(z_, q) for z_ in z_peers for q in (1 - k, k)] + [(z, 1 - k)]

    dual = jnp.zeros((blocks, wide), jnp.float32)
    for it in range(ITERS):
        top, total = row_stats(dual)
        row_dual = -(top + jnp.log2(total))
        for c in range(blocks):
            t = row_dual - tile(c)
            top = jnp.max(t, axis=0, keepdims=True)
            total = jnp.sum(jnp.exp2(t - top), axis=0, keepdims=True)
            ex[it, own_e, c:c + 1] = top + jnp.log2(total)
        here = ex.at[it, own_e]

        for zt, kt in e_peers:
            send(here, here, e_s.at[it], e_r.at[it], at(zt, b, l * 2 + kt))
        others = ex.at[it, pl.ds(0, 2 * nz - 1)]
        gone(others, e_s.at[it])
        if it == ITERS - 1:
            passed = pw.at[1 - h, k]
            came(passed, p_r.at[1])
            send(passed, passed, p_s.at[2], p_r.at[2], neighbour)
            gone(passed, p_s.at[2])
        came(others, e_r.at[it])
        parts = ex[it]
        top = jnp.max(parts, axis=0)
        total = jnp.sum(jnp.exp2(parts - top[None]), axis=0)
        dual = -(top + jnp.log2(total))

    urow[...] = dual
    count = nl // 2
    start = h * count
    top, total = row_stats(dual, start, count)
    weights = []
    for half in range(2):
        at_x = half * nx + x
        t = urow[pl.ds(at_x, 1)] - g[pl.ds(at_x * nl + start, count)].reshape(count * rows, wide)
        weights.append((jnp.exp2(t - top) / total).astype(jnp.bfloat16))

    came(pw.at[h, 1 - k], p_r.at[0])
    came(pw.at[1 - h, 1 - k], p_r.at[2])
    for kk in range(2):
        coupled = jnp.dot(weights[0], pw[0, kk].reshape(wide, depth), preferred_element_type=jnp.float32)
        coupled += jnp.dot(weights[1], pw[1, kk].reshape(wide, depth), preferred_element_type=jnp.float32)
        for i in range(count):
            piece = turn(coupled[i * rows:(i + 1) * rows], patches).astype(jnp.bfloat16)
            pb[i * nv:(i + 1) * nv, kk] = piece.reshape(nv, st, width)

    parity = lax.rem(x, 2)
    slot = x * nl + l
    for vt in v_peers + [v]:
        for i in range(count):
            src, dst, xt = pb.at[i * nv + vt], rp.at[slot], 2 * i + k
            if vt is not v:
                send(src, dst, c_s, c_r, at(z, h * nx + xt, vt))
            else:

                @pl.when(xt != x)
                def _():
                    send(src, dst, c_s, c_r, at(z, h * nx + xt, vt))

    @pl.when(parity == k)
    def _():
        rp[slot] = pb[x // 2 * nv + v]

    finish()
    lane = lax.broadcasted_iota(jnp.int32, (st, width), 1) & (rows - 1)
    time = jnp.zeros((st, width), jnp.float32)
    for i in range(rows):
        time = jnp.where(lane == i, times[i], time)
    clip_of = lax.broadcasted_iota(jnp.int32, (rows, st, width), 0)
    keep = (lax.broadcasted_iota(jnp.int32, (rows, st, width), 2) & (rows - 1)) == clip_of
    from_lane = lax.broadcasted_iota(jnp.int32, (width, nv * patches), 0) // rows
    to_patch = lax.broadcasted_iota(jnp.int32, (width, nv * patches), 1)
    came(la.at[pl.ds(0, nv - 1)], a_r)
    number = nx * nl

    @pl.when(parity == k)
    def _():
        came(rp.at[pl.ds(0, number - 1)], c_r)

    @pl.when(parity != k)
    def _():
        came(rp, c_r)

    made = jnp.zeros((rows * st, nv * patches), jnp.float32)
    for j in range(nv):
        coupled = rp[j // 2, j % 2].astype(jnp.float32)
        for xt in range(1, nx):
            coupled = coupled + rp[xt * nl + j // 2, j % 2].astype(jnp.float32)
        mixed = (1.0 - time) * la[j].astype(jnp.float32) + time * coupled
        spread = jnp.where(keep, mixed[None], 0.0).reshape(rows * st, width).astype(jnp.bfloat16)
        pick = jnp.where(to_patch == from_lane + j * patches, 1.0, 0.0).astype(jnp.bfloat16)
        made = made + jnp.dot(spread, pick, preferred_element_type=jnp.float32)
    out[...] = made.astype(jnp.bfloat16)

    @pl.when(parity == k)
    def _():
        gone(pb.at[pl.ds(0, number - 1)], c_s)
        finish()

    @pl.when(parity != k)
    def _():
        gone(pb, c_s)
        finish()


def on_device(nc, nv, latents, noise, offsets, times, embed):
    nb = nv
    nz, nl, nx = nc // nb, nv // 2, nb // 2
    rows, depth = latents.shape
    patches = depth // S
    st = S // nv
    wide = nz * rows
    width = patches * rows
    f32, bf16 = jnp.float32, jnp.bfloat16
    vmem = pl.BlockSpec(memory_space=pltpu.VMEM)
    sems = []
    for shape in (1, 1, 1, 1, 1, 1, 1, 1, 1, ITERS, ITERS, 1, 1, 1, 1, 3, 3, 4):
        sems.append(pltpu.SemaphoreType.DMA if shape == 1 else pltpu.SemaphoreType.DMA((shape,)))
    tokens = pl.pallas_call(
        functools.partial(couple, nz, nb, nv),
        out_shape=jax.ShapeDtypeStruct((rows * st, nv * patches), bf16),
        in_specs=[pl.BlockSpec(memory_space=pltpu.HBM)] * 4,
        out_specs=vmem,
        scratch_shapes=[
            pltpu.VMEM((rows, depth), bf16),
            pltpu.VMEM((rows, depth), bf16),
            pltpu.SMEM((4, rows), jnp.int32),
            pltpu.SMEM((rows,), f32),
            pltpu.VMEM((2, 2, nz, rows, depth), bf16),
            pltpu.VMEM((nb, rows, depth), bf16),
            pltpu.VMEM((nb, rows, wide), f32),
            pltpu.VMEM((nv, rows, wide), f32),
            pltpu.VMEM((nb * nl, rows, wide), f32),
            pltpu.VMEM((ITERS, 2 * nz, nb, wide), f32),
            pltpu.VMEM((nb, wide), f32),
            pltpu.VMEM((nl // 2 * nv, 2, st, width), bf16),
            pltpu.VMEM((nx * nl, 2, st, width), bf16),
            pltpu.VMEM((nv, st, width), bf16),
            pltpu.VMEM((nv, st, width), bf16),
            *sems,
        ],
        compiler_params=pltpu.CompilerParams(
            collective_id=0, has_side_effects=True, vmem_limit_bytes=VMEM
        ),
        name="couple",
    )(*[
        pltpu.with_memory_space_constraint(a, pltpu.HBM)
        for a in (latents, noise, offsets.reshape(rows, 4).T, times)
    ])
    made = jnp.dot(tokens, embed, preferred_element_type=f32).astype(bf16)
    return made.reshape(rows, st, embed.shape[1])


def solution(mesh):
    placed = (P("clip", "val"), P("clip", "val"), P("clip", None, None), P("clip"), P())
    return jax.shard_map(
        functools.partial(on_device, mesh.shape["clip"], mesh.shape["val"]),
        mesh=mesh,
        in_specs=placed,
        out_specs=P("clip", "val", None),
        check_vma=False,
    )
```

```python
import functools
import math

import jax
import jax.numpy as jnp
from jax import lax
from jax.experimental import pallas as pl
from jax.experimental.pallas import tpu as pltpu
from jax.sharding import PartitionSpec as P

P_SIZE = 64
FR = 2
GW = 16
GH = 4
ITERS = 4
VMEM = 16 << 20
S = FR * GH * GW
LOG2E = 1.4426950408889634


def ring(n):
    return sorted(range(1, n), key=lambda i: -min(i, n - i))


def turn(x, patches):
    return jnp.concatenate([x[:, p * S:(p + 1) * S] for p in range(patches)], axis=0).T


def couple(nz, nb, nv, lat_in, noise_in, off_in, times_in, out, lat, noise, off, times, pw, lg, part, rv, g, ex, urow, pb, rp, ms, la,
           w_s, w_r, l_s, l_near, l_far, r_s, r_r, g_s, g_r, e_s, e_r, c_s, c_r, a_s, a_r, p_s, p_r, i_s, f_s, f_r):
    nl, nx = nv // 2, nb // 2
    rows, depth = lat.shape
    patches = depth // S
    wide = nz * rows
    n = nb * wide
    st = S // nv
    width = patches * rows
    clip = lax.axis_index("clip")
    v = lax.axis_index("val")
    z, b = clip // nb, lax.rem(clip, nb)
    h, x = b // nx, lax.rem(b, nx)
    l, k = v // 2, lax.rem(v, 2)
    y = h * nl + l
    left = []

    def at(z_, b_, v_):
        return {"clip": z_ * nb + b_, "val": v_}

    def send(src, dst, s_sem, r_sem, where):
        pltpu.make_async_remote_copy(src, dst, s_sem, r_sem, device_id=where).start()

    def came(like, sem):
        pltpu.make_async_remote_copy(like, like, sem, sem, device_id=at(z, b, v)).wait_recv()

    def gone(like, sem):
        left.append(lambda: pltpu.make_async_remote_copy(like, like, sem, sem, device_id=at(z, b, v)).wait_send())

    def finish():
        while left:
            left.pop()()

    z_peers = [lax.rem(z + i, nz) for i in ring(nz)]
    far_peers = [(1 - h) * nx + lax.rem(x + i, nx) for i in ring(nx) + [0]]
    near_peers = [h * nx + lax.rem(x + i, nx) for i in ring(nx)]
    v_peers = [lax.rem(v + i, nv) for i in range(1, nv)]

    barrier = pltpu.get_barrier_semaphore()
    for bt in far_peers + near_peers:
        pl.semaphore_signal(barrier, inc=1, device_id=at(z, bt, v))
    for zt in z_peers:
        pl.semaphore_signal(barrier, inc=1, device_id=at(zt, b, v))
    for vt in v_peers:
        pl.semaphore_signal(barrier, inc=1, device_id=at(z, b, vt))

    loads = [
        pltpu.make_async_copy(src, dst, i_s.at[i])
        for i, (src, dst) in enumerate(((off_in, off), (noise_in, noise), (lat_in, lat), (times_in, times)))
    ]
    for load in loads:
        load.start()

    rowi = lax.broadcasted_iota(jnp.int32, (rows, S), 0)
    lane = lax.broadcasted_iota(jnp.int32, (rows, S), 1)
    first = lane < GH * GW
    sy = jnp.zeros((rows, S), jnp.int32)
    sx = jnp.zeros((rows, S), jnp.int32)
    loads[0].wait()
    for i in range(rows):
        here = rowi == i
        sy = jnp.where(here, jnp.where(first, off[0, i], off[2, i]), sy)
        sx = jnp.where(here, jnp.where(first, off[1, i], off[3, i]), sx)
    col = lane & (GW - 1)
    row = (lane // GW) & (GH - 1)
    loads[1].wait()
    for p in range(patches):
        t = noise[:, p * S:(p + 1) * S].astype(jnp.float32)
        for bit in (1, 2, 4, 8):
            turned = jnp.where(col >= bit, pltpu.roll(t, bit, 1), pltpu.roll(t, S - GW + bit, 1))
            t = jnp.where((sx & bit) != 0, turned, t)
        for bit in (1, 2):
            turned = jnp.where(
                row >= bit, pltpu.roll(t, bit * GW, 1), pltpu.roll(t, S - GH * GW + bit * GW, 1)
            )
            t = jnp.where((sy & bit) != 0, turned, t)
        pw[h, k, z, :, p * S:(p + 1) * S] = t.astype(jnp.bfloat16)
    loads[2].wait()
    loads[3].wait()
    lg[b] = lat[...]
    pl.semaphore_wait(barrier, (nz - 1) + (nb - 1) + (nv - 1))

    for bt in far_peers:
        send(lat, lg.at[b], l_s, l_far, at(z, bt, v))
    for bt in near_peers:
        send(lat, lg.at[b], l_s, l_near, at(z, bt, v))
    gone(lg.at[pl.ds(0, nb - 1)], l_s)
    mine = pw.at[h, k, z]
    for zt in z_peers:
        send(mine, mine, w_s, w_r, at(zt, b, v))
    if nz > 1:
        gone(pw.at[h, k, pl.ds(0, nz - 1)], w_s)

    ms[...] = turn(lat[...].astype(jnp.float32), patches).astype(jnp.bfloat16).reshape(nv, st, width)
    for vt in v_peers:
        send(ms.at[vt], la.at[v], a_s, a_r, at(z, b, vt))
    gone(ms.at[pl.ds(0, nv - 1)], a_s)
    la[v] = ms[v]

    if nz > 1:
        came(pw.at[h, k, pl.ds(0, nz - 1)], w_r)
    neighbour = at(z, b, l * 2 + (1 - k))
    facing = at(z, (1 - h) * nx + x, v)
    panel = pw.at[h, k]
    send(panel, panel, p_s.at[0], p_r.at[0], neighbour)
    gone(panel, p_s.at[0])
    noises = pw[h, k].reshape(wide, depth)
    square = noises.astype(jnp.float32)
    square = jnp.sum(square * square, axis=1, keepdims=True)
    diagonal = lax.broadcasted_iota(jnp.int32, (wide, wide), 0) == lax.broadcasted_iota(
        jnp.int32, (wide, wide), 1
    )
    square = jnp.sum(jnp.where(diagonal, square, 0.0), axis=0, keepdims=True)

    def block(half):
        gram = lax.dot_general(
            lg[pl.ds(half * nx, nx)].reshape(nx * rows, depth),
            pw[h, k].reshape(wide, depth),
            (((1,), (1,)), ((), ())),
            preferred_element_type=jnp.float32,
        )
        part[pl.ds(half * nx, nx)] = (square - 2.0 * gram).reshape(nx, rows, wide)

    def r_send(half):
        for i in range(nx):
            vt = half * nx + lax.rem(x + i, nx)

            @pl.when(vt != v)
            def _():
                send(part.at[vt], rv.at[v], r_s, r_r, at(z, b, vt))

    came(lg.at[pl.ds(0, nx - 1)], l_near)
    block(h)
    r_send(h)
    came(lg.at[pl.ds(0, nx)], l_far)
    block(1 - h)
    r_send(1 - h)
    gone(part.at[pl.ds(0, nv - 1)], r_s)
    rv[v] = part[v]
    came(rv.at[pl.ds(0, nv - 1)], r_r)
    volume = float(nv * depth)
    entropy = 0.5 / math.sqrt(volume)

    piece = g.at[b * nl + l]
    piece[...] = jnp.sum(rv[...], axis=0) * (LOG2E / (volume * entropy))

    ny = 2 * nl
    x_peers = [lax.rem(x + i, nx) for i in ring(nx)]

    def pass_on(h_, l_):
        here = g.at[(h_ * nx + x) * nl + l_]
        for xt in x_peers:
            send(here, here, f_s, f_r, at(z, h * nx + xt, v))

    for i in ring(ny):
        yt = lax.rem(y + i, ny)
        send(piece, piece, g_s, g_r.at[i], at(z, yt // nl * nx + x, lax.rem(yt, nl) * 2 + k))
    pass_on(h, l)
    for i in reversed(ring(ny)):
        yt = lax.rem(y + ny - i, ny)
        came(piece, g_r.at[i])
        pass_on(yt // nl, lax.rem(yt, nl))
    gone(g.at[pl.ds(0, ny - 1)], g_s)
    pieces = g.at[pl.ds(0, ny * (nx - 1))]
    gone(pieces, f_s)
    came(pieces, f_r)
    send(panel, panel, p_s.at[1], p_r.at[1], facing)
    gone(panel, p_s.at[1])

    blocks = nb
    own_e = z * 2 + k

    def tile(c, first=0, count=nl):
        return g[pl.ds(c * nl + first, count)].reshape(count * rows, wide)

    def row_stats(dual, first=0, count=nl):
        top = dual[0:1] - tile(0, first, count)
        for c in range(1, blocks):
            top = jnp.maximum(top, dual[c:c + 1] - tile(c, first, count))
        top = jnp.max(top, axis=1, keepdims=True)
        total = jnp.exp2(dual[0:1] - tile(0, first, count) - top)
        for c in range(1, blocks):
            total = total + jnp.exp2(dual[c:c + 1] - tile(c, first, count) - top)
        return top, jnp.sum(total, axis=1, keepdims=True)

    e_peers = [(z_, q) for z_ in z_peers for q in (1 - k, k)] + [(z, 1 - k)]

    dual = jnp.zeros((blocks, wide), jnp.float32)
    for it in range(ITERS):
        top, total = row_stats(dual)
        row_dual = -(top + jnp.log2(total))
        for c in range(blocks):
            t = row_dual - tile(c)
            top = jnp.max(t, axis=0, keepdims=True)
            total = jnp.sum(jnp.exp2(t - top), axis=0, keepdims=True)
            ex[it, own_e, c:c + 1] = top + jnp.log2(total)
        here = ex.at[it, own_e]

        for zt, kt in e_peers:
            send(here, here, e_s.at[it], e_r.at[it], at(zt, b, l * 2 + kt))
        others = ex.at[it, pl.ds(0, 2 * nz - 1)]
        gone(others, e_s.at[it])
        if it == ITERS - 1:
            passed = pw.at[1 - h, k]
            came(passed, p_r.at[1])
            send(passed, passed, p_s.at[2], p_r.at[2], neighbour)
            gone(passed, p_s.at[2])
        came(others, e_r.at[it])
        parts = ex[it]
        top = jnp.max(parts, axis=0)
        total = jnp.sum(jnp.exp2(parts - top[None]), axis=0)
        dual = -(top + jnp.log2(total))

    urow[...] = dual
    count = nl // 2
    start = h * count
    top, total = row_stats(dual, start, count)
    weights = []
    for half in range(2):
        at_x = half * nx + x
        t = urow[pl.ds(at_x, 1)] - g[pl.ds(at_x * nl + start, count)].reshape(count * rows, wide)
        weights.append((jnp.exp2(t - top) / total).astype(jnp.bfloat16))

    came(pw.at[h, 1 - k], p_r.at[0])
    came(pw.at[1 - h, 1 - k], p_r.at[2])
    parity = lax.rem(x, 2)
    slot = l * nx + x
    partial = []
    for kk in range(2):
        coupled = jnp.dot(weights[0], pw[0, kk].reshape(wide, depth), preferred_element_type=jnp.float32)
        partial.append(
            coupled + jnp.dot(weights[1], pw[1, kk].reshape(wide, depth), preferred_element_type=jnp.float32)
        )

    for i in range(count):
        for kk in range(2):
            made = turn(partial[kk][i * rows:(i + 1) * rows], patches).astype(jnp.bfloat16)
            pb[i * nv:(i + 1) * nv, kk] = made.reshape(nv, st, width)
        xt = 2 * i + k
        for vt in v_peers:
            send(pb.at[i * nv + vt], rp.at[slot], c_s, c_r.at[l], at(z, h * nx + xt, vt))

        @pl.when(xt != x)
        def _():
            send(pb.at[i * nv + v], rp.at[slot], c_s, c_r.at[l], at(z, h * nx + xt, v))

    @pl.when(parity == k)
    def _():
        rp[slot] = pb[x // 2 * nv + v]

    finish()
    lane = lax.broadcasted_iota(jnp.int32, (st, width), 1) & (rows - 1)
    time = jnp.zeros((st, width), jnp.float32)
    for i in range(rows):
        time = jnp.where(lane == i, times[i], time)
    clip_of = lax.broadcasted_iota(jnp.int32, (rows, st, width), 0)
    keep = (lax.broadcasted_iota(jnp.int32, (rows, st, width), 2) & (rows - 1)) == clip_of
    from_lane = lax.broadcasted_iota(jnp.int32, (width, nv * patches), 0) // rows
    to_patch = lax.broadcasted_iota(jnp.int32, (width, nv * patches), 1)
    came(la.at[pl.ds(0, nv - 1)], a_r)
    number = nx * nl
    made = jnp.zeros((rows * st, nv * patches), jnp.float32)
    for i in range(nl):
        lt = lax.rem(l + i, nl)
        if i == 0:

            @pl.when(parity == k)
            def _():
                came(rp.at[pl.ds(0, nx - 1)], c_r.at[lt])

            @pl.when(parity != k)
            def _():
                came(rp.at[pl.ds(0, nx)], c_r.at[lt])

        else:
            came(rp.at[pl.ds(0, nx)], c_r.at[lt])
        for kk in range(2):
            coupled = rp[lt * nx, kk].astype(jnp.float32)
            for xt in range(1, nx):
                coupled = coupled + rp[lt * nx + xt, kk].astype(jnp.float32)
            mixed = (1.0 - time) * la[lt * 2 + kk].astype(jnp.float32) + time * coupled
            spread = jnp.where(keep, mixed[None], 0.0).reshape(rows * st, width).astype(jnp.bfloat16)
            start = (lt * 2 + kk) * patches
            pick = jnp.where(to_patch == from_lane + start, 1.0, 0.0).astype(jnp.bfloat16)
            made = made + jnp.dot(spread, pick, preferred_element_type=jnp.float32)
    out[...] = made.astype(jnp.bfloat16)

    @pl.when(parity == k)
    def _():
        gone(pb.at[pl.ds(0, number - 1)], c_s)
        finish()

    @pl.when(parity != k)
    def _():
        gone(pb, c_s)
        finish()


def on_device(nc, nv, latents, noise, offsets, times, embed):
    nb = nv
    nz, nl, nx = nc // nb, nv // 2, nb // 2
    rows, depth = latents.shape
    patches = depth // S
    st = S // nv
    wide = nz * rows
    width = patches * rows
    f32, bf16 = jnp.float32, jnp.bfloat16
    vmem = pl.BlockSpec(memory_space=pltpu.VMEM)
    sems = []
    for shape in (1, 1, 1, 1, 1, 1, 1, 1, 2 * nl, ITERS, ITERS, 1, nl, 1, 1, 3, 3, 4, 1, 1):
        sems.append(pltpu.SemaphoreType.DMA if shape == 1 else pltpu.SemaphoreType.DMA((shape,)))
    tokens = pl.pallas_call(
        functools.partial(couple, nz, nb, nv),
        out_shape=jax.ShapeDtypeStruct((rows * st, nv * patches), bf16),
        in_specs=[pl.BlockSpec(memory_space=pltpu.HBM)] * 4,
        out_specs=vmem,
        scratch_shapes=[
            pltpu.VMEM((rows, depth), bf16),
            pltpu.VMEM((rows, depth), bf16),
            pltpu.SMEM((4, rows), jnp.int32),
            pltpu.SMEM((rows,), f32),
            pltpu.VMEM((2, 2, nz, rows, depth), bf16),
            pltpu.VMEM((nb, rows, depth), bf16),
            pltpu.VMEM((nb, rows, wide), f32),
            pltpu.VMEM((nv, rows, wide), f32),
            pltpu.VMEM((nb * nl, rows, wide), f32),
            pltpu.VMEM((ITERS, 2 * nz, nb, wide), f32),
            pltpu.VMEM((nb, wide), f32),
            pltpu.VMEM((nl // 2 * nv, 2, st, width), bf16),
            pltpu.VMEM((nx * nl, 2, st, width), bf16),
            pltpu.VMEM((nv, st, width), bf16),
            pltpu.VMEM((nv, st, width), bf16),
            *sems,
        ],
        compiler_params=pltpu.CompilerParams(
            collective_id=0, has_side_effects=True, vmem_limit_bytes=VMEM
        ),
        name="couple",
    )(*[
        pltpu.with_memory_space_constraint(a, pltpu.HBM)
        for a in (latents, noise, offsets.reshape(rows, 4).T, times)
    ])
    made = jnp.dot(tokens, embed, preferred_element_type=f32).astype(bf16)
    return made.reshape(rows, st, embed.shape[1])


def solution(mesh):
    placed = (P("clip", "val"), P("clip", "val"), P("clip", None, None), P("clip"), P())
    return jax.shard_map(
        functools.partial(on_device, mesh.shape["clip"], mesh.shape["val"]),
        mesh=mesh,
        in_specs=placed,
        out_specs=P("clip", "val", None),
        check_vma=False,
    )
```

```python
import functools
import math

import jax
import jax.numpy as jnp
from jax import lax
from jax.experimental import pallas as pl
from jax.experimental.pallas import tpu as pltpu
from jax.sharding import PartitionSpec as P

P_SIZE = 64
FR = 2
GW = 16
GH = 4
ITERS = 4
VMEM = 16 << 20
S = FR * GH * GW
LOG2E = 1.4426950408889634


def ring(n):
    return sorted(range(1, n), key=lambda i: -min(i, n - i))


def turn(x, patches):
    return jnp.concatenate([x[:, p * S:(p + 1) * S] for p in range(patches)], axis=0).T


def couple(nz, nb, nv, lat_in, noise_in, off_in, times_in, out, lat, noise, off, times, pw, lg, part, rv, g, ex, urow, pb, rp, ms, la,
           w_s, w_r, l_s, l_near, l_far, r_s, r_r, g_s, g_r, e_s, e_r, c_s, c_r, a_s, a_r, p_s, p_r, i_s, f_s, f_r, l_face, k_s):
    nl, nx = nv // 2, nb // 2
    rows, depth = lat.shape
    patches = depth // S
    wide = nz * rows
    n = nb * wide
    st = S // nv
    width = patches * rows
    clip = lax.axis_index("clip")
    v = lax.axis_index("val")
    z, b = clip // nb, lax.rem(clip, nb)
    h, x = b // nx, lax.rem(b, nx)
    l, k = v // 2, lax.rem(v, 2)
    y = h * nl + l
    left = []

    def at(z_, b_, v_):
        return {"clip": z_ * nb + b_, "val": v_}

    def send(src, dst, s_sem, r_sem, where):
        pltpu.make_async_remote_copy(src, dst, s_sem, r_sem, device_id=where).start()

    def came(like, sem):
        pltpu.make_async_remote_copy(like, like, sem, sem, device_id=at(z, b, v)).wait_recv()

    def gone(like, sem):
        left.append(lambda: pltpu.make_async_remote_copy(like, like, sem, sem, device_id=at(z, b, v)).wait_send())

    def finish():
        while left:
            left.pop()()

    z_peers = [lax.rem(z + i, nz) for i in ring(nz)]
    far = (1 - h) * nx + x
    near_peers = [h * nx + lax.rem(x + i, nx) for i in ring(nx)]
    l_others = [nl - 1 - l] if nl == 2 else [nl - 1 - l, lax.rem(l + 2, 4), l + 1 - 2 * lax.rem(l, 2)]
    v_peers = [lt * 2 + kt for lt in l_others for kt in (1 - k, k)] + [l * 2 + (1 - k)]

    barrier = pltpu.get_barrier_semaphore()
    for bt in [far] + near_peers:
        pl.semaphore_signal(barrier, inc=1, device_id=at(z, bt, v))
    for zt in z_peers:
        pl.semaphore_signal(barrier, inc=1, device_id=at(zt, b, v))
    for vt in v_peers:
        pl.semaphore_signal(barrier, inc=1, device_id=at(z, b, vt))

    loads = [
        pltpu.make_async_copy(src, dst, i_s.at[i])
        for i, (src, dst) in enumerate(((off_in, off), (noise_in, noise), (lat_in, lat), (times_in, times)))
    ]
    for load in loads:
        load.start()

    rowi = lax.broadcasted_iota(jnp.int32, (rows, S), 0)
    lane = lax.broadcasted_iota(jnp.int32, (rows, S), 1)
    first = lane < GH * GW
    sy = jnp.zeros((rows, S), jnp.int32)
    sx = jnp.zeros((rows, S), jnp.int32)
    loads[0].wait()
    for i in range(rows):
        here = rowi == i
        sy = jnp.where(here, jnp.where(first, off[0, i], off[2, i]), sy)
        sx = jnp.where(here, jnp.where(first, off[1, i], off[3, i]), sx)
    col = lane & (GW - 1)
    row = (lane // GW) & (GH - 1)
    loads[1].wait()
    for p in range(patches):
        t = noise[:, p * S:(p + 1) * S].astype(jnp.float32)
        for bit in (1, 2, 4, 8):
            turned = jnp.where(col >= bit, pltpu.roll(t, bit, 1), pltpu.roll(t, S - GW + bit, 1))
            t = jnp.where((sx & bit) != 0, turned, t)
        for bit in (1, 2):
            turned = jnp.where(
                row >= bit, pltpu.roll(t, bit * GW, 1), pltpu.roll(t, S - GH * GW + bit * GW, 1)
            )
            t = jnp.where((sy & bit) != 0, turned, t)
        pw[h, k, z, :, p * S:(p + 1) * S] = t.astype(jnp.bfloat16)
    loads[2].wait()
    loads[3].wait()
    lg[b] = lat[...]
    pl.semaphore_wait(barrier, (nz - 1) + nx + (nv - 1))

    facing = at(z, far, v)
    send(lat, lg.at[b], l_s, l_face, facing)
    for bt in near_peers:
        send(lat, lg.at[b], l_s, l_near, at(z, bt, v))
    gone(lg.at[pl.ds(0, nx)], l_s)
    mine = pw.at[h, k, z]
    for zt in z_peers:
        send(mine, mine, w_s, w_r, at(zt, b, v))
    if nz > 1:
        gone(pw.at[h, k, pl.ds(0, nz - 1)], w_s)

    ms[...] = turn(lat[...].astype(jnp.float32), patches).astype(jnp.bfloat16).reshape(nv, st, width)
    for vt in v_peers:
        send(ms.at[vt], la.at[v], a_s, a_r, at(z, b, vt))
    gone(ms.at[pl.ds(0, nv - 1)], a_s)
    la[v] = ms[v]
    came(lat, l_face)
    for bt in near_peers:
        send(lg.at[far], lg.at[far], k_s, l_far, at(z, bt, v))
    gone(lg.at[pl.ds(0, nx - 1)], k_s)

    if nz > 1:
        came(pw.at[h, k, pl.ds(0, nz - 1)], w_r)
    neighbour = at(z, b, l * 2 + (1 - k))
    panel = pw.at[h, k]
    noises = pw[h, k].reshape(wide, depth)
    square = noises.astype(jnp.float32)
    square = jnp.sum(square * square, axis=1, keepdims=True)
    diagonal = lax.broadcasted_iota(jnp.int32, (wide, wide), 0) == lax.broadcasted_iota(
        jnp.int32, (wide, wide), 1
    )
    square = jnp.sum(jnp.where(diagonal, square, 0.0), axis=0, keepdims=True)

    def block(half):
        gram = lax.dot_general(
            lg[pl.ds(half * nx, nx)].reshape(nx * rows, depth),
            pw[h, k].reshape(wide, depth),
            (((1,), (1,)), ((), ())),
            preferred_element_type=jnp.float32,
        )
        part[pl.ds(half * nx, nx)] = (square - 2.0 * gram).reshape(nx, rows, wide)

    def r_send(half):
        for i in range(nx):
            vt = half * nx + lax.rem(x + i, nx)

            @pl.when(vt != v)
            def _():
                send(part.at[vt], rv.at[v], r_s, r_r, at(z, b, vt))

    came(lg.at[pl.ds(0, nx - 1)], l_near)
    block(h)
    r_send(h)
    came(lg.at[pl.ds(0, nx - 1)], l_far)
    block(1 - h)
    r_send(1 - h)
    gone(part.at[pl.ds(0, nv - 1)], r_s)
    rv[v] = part[v]
    came(rv.at[pl.ds(0, nv - 1)], r_r)
    volume = float(nv * depth)
    entropy = 0.5 / math.sqrt(volume)

    piece = g.at[b * nl + l]
    piece[...] = jnp.sum(rv[...], axis=0) * (LOG2E / (volume * entropy))

    ny = 2 * nl
    x_peers = [lax.rem(x + i, nx) for i in ring(nx)]

    def pass_on(h_, l_):
        here = g.at[(h_ * nx + x) * nl + l_]
        for xt in x_peers:
            send(here, here, f_s, f_r, at(z, h * nx + xt, v))

    for i in ring(ny):
        yt = lax.rem(y + i, ny)
        send(piece, piece, g_s, g_r.at[i], at(z, yt // nl * nx + x, lax.rem(yt, nl) * 2 + k))
    pass_on(h, l)
    for i in reversed(ring(ny)):
        yt = lax.rem(y + ny - i, ny)
        came(piece, g_r.at[i])
        pass_on(yt // nl, lax.rem(yt, nl))
    gone(g.at[pl.ds(0, ny - 1)], g_s)
    pieces = g.at[pl.ds(0, ny * (nx - 1))]
    gone(pieces, f_s)
    came(pieces, f_r)
    send(panel, panel, p_s.at[0], p_r.at[0], neighbour)
    gone(panel, p_s.at[0])
    send(panel, panel, p_s.at[1], p_r.at[1], facing)
    gone(panel, p_s.at[1])

    blocks = nb
    own_e = z * 2 + k

    def tile(c, first=0, count=nl):
        return g[pl.ds(c * nl + first, count)].reshape(count * rows, wide)

    def row_stats(dual, first=0, count=nl):
        top = dual[0:1] - tile(0, first, count)
        for c in range(1, blocks):
            top = jnp.maximum(top, dual[c:c + 1] - tile(c, first, count))
        top = jnp.max(top, axis=1, keepdims=True)
        total = jnp.exp2(dual[0:1] - tile(0, first, count) - top)
        for c in range(1, blocks):
            total = total + jnp.exp2(dual[c:c + 1] - tile(c, first, count) - top)
        return top, jnp.sum(total, axis=1, keepdims=True)

    e_peers = [(z_, q) for z_ in z_peers for q in (1 - k, k)] + [(z, 1 - k)]

    dual = jnp.zeros((blocks, wide), jnp.float32)
    for it in range(ITERS):
        top, total = row_stats(dual)
        row_dual = -(top + jnp.log2(total))
        for c in range(blocks):
            t = row_dual - tile(c)
            top = jnp.max(t, axis=0, keepdims=True)
            total = jnp.sum(jnp.exp2(t - top), axis=0, keepdims=True)
            ex[it, own_e, c:c + 1] = top + jnp.log2(total)
        here = ex.at[it, own_e]

        for zt, kt in e_peers:
            send(here, here, e_s.at[it], e_r.at[it], at(zt, b, l * 2 + kt))
        others = ex.at[it, pl.ds(0, 2 * nz - 1)]
        gone(others, e_s.at[it])
        if it == ITERS - 1:
            passed = pw.at[1 - h, k]
            came(passed, p_r.at[1])
            send(passed, passed, p_s.at[2], p_r.at[2], neighbour)
            gone(passed, p_s.at[2])
        came(others, e_r.at[it])
        parts = ex[it]
        top = jnp.max(parts, axis=0)
        total = jnp.sum(jnp.exp2(parts - top[None]), axis=0)
        dual = -(top + jnp.log2(total))

    urow[...] = dual
    count = nl // 2
    start = h * count
    top, total = row_stats(dual, start, count)
    weights = []
    for half in range(2):
        at_x = half * nx + x
        t = urow[pl.ds(at_x, 1)] - g[pl.ds(at_x * nl + start, count)].reshape(count * rows, wide)
        weights.append((jnp.exp2(t - top) / total).astype(jnp.bfloat16))

    came(pw.at[h, 1 - k], p_r.at[0])
    came(pw.at[1 - h, 1 - k], p_r.at[2])
    parity = lax.rem(x, 2)
    slot = l * nx + x
    partial = []
    for kk in range(2):
        coupled = jnp.dot(weights[0], pw[0, kk].reshape(wide, depth), preferred_element_type=jnp.float32)
        partial.append(
            coupled + jnp.dot(weights[1], pw[1, kk].reshape(wide, depth), preferred_element_type=jnp.float32)
        )

    for i in range(count):
        for kk in range(2):
            made = turn(partial[kk][i * rows:(i + 1) * rows], patches).astype(jnp.bfloat16)
            pb[i * nv:(i + 1) * nv, kk] = made.reshape(nv, st, width)
        xt = 2 * i + k
        for vt in v_peers:
            send(pb.at[i * nv + vt], rp.at[slot], c_s, c_r.at[l], at(z, h * nx + xt, vt))

        @pl.when(xt != x)
        def _():
            send(pb.at[i * nv + v], rp.at[slot], c_s, c_r.at[l], at(z, h * nx + xt, v))

    @pl.when(parity == k)
    def _():
        rp[slot] = pb[x // 2 * nv + v]

    finish()
    lane = lax.broadcasted_iota(jnp.int32, (st, width), 1) & (rows - 1)
    time = jnp.zeros((st, width), jnp.float32)
    for i in range(rows):
        time = jnp.where(lane == i, times[i], time)
    clip_of = lax.broadcasted_iota(jnp.int32, (rows, st, width), 0)
    keep = (lax.broadcasted_iota(jnp.int32, (rows, st, width), 2) & (rows - 1)) == clip_of
    from_lane = lax.broadcasted_iota(jnp.int32, (width, nv * patches), 0) // rows
    to_patch = lax.broadcasted_iota(jnp.int32, (width, nv * patches), 1)
    came(la.at[pl.ds(0, nv - 1)], a_r)
    number = nx * nl
    made = jnp.zeros((rows * st, nv * patches), jnp.float32)
    for i, lt in enumerate([l] + l_others[::-1]):
        if i == 0:

            @pl.when(parity == k)
            def _():
                came(rp.at[pl.ds(0, nx - 1)], c_r.at[lt])

            @pl.when(parity != k)
            def _():
                came(rp.at[pl.ds(0, nx)], c_r.at[lt])

        else:
            came(rp.at[pl.ds(0, nx)], c_r.at[lt])
        for kk in range(2):
            coupled = rp[lt * nx, kk].astype(jnp.float32)
            for xt in range(1, nx):
                coupled = coupled + rp[lt * nx + xt, kk].astype(jnp.float32)
            mixed = (1.0 - time) * la[lt * 2 + kk].astype(jnp.float32) + time * coupled
            spread = jnp.where(keep, mixed[None], 0.0).reshape(rows * st, width).astype(jnp.bfloat16)
            start = (lt * 2 + kk) * patches
            pick = jnp.where(to_patch == from_lane + start, 1.0, 0.0).astype(jnp.bfloat16)
            made = made + jnp.dot(spread, pick, preferred_element_type=jnp.float32)
    out[...] = made.astype(jnp.bfloat16)

    @pl.when(parity == k)
    def _():
        gone(pb.at[pl.ds(0, number - 1)], c_s)
        finish()

    @pl.when(parity != k)
    def _():
        gone(pb, c_s)
        finish()


def on_device(nc, nv, latents, noise, offsets, times, embed):
    nb = nv
    nz, nl, nx = nc // nb, nv // 2, nb // 2
    rows, depth = latents.shape
    patches = depth // S
    st = S // nv
    wide = nz * rows
    width = patches * rows
    f32, bf16 = jnp.float32, jnp.bfloat16
    vmem = pl.BlockSpec(memory_space=pltpu.VMEM)
    sems = []
    for shape in (1, 1, 1, 1, 1, 1, 1, 1, 2 * nl, ITERS, ITERS, 1, nl, 1, 1, 3, 3, 4, 1, 1, 1, 1):
        sems.append(pltpu.SemaphoreType.DMA if shape == 1 else pltpu.SemaphoreType.DMA((shape,)))
    tokens = pl.pallas_call(
        functools.partial(couple, nz, nb, nv),
        out_shape=jax.ShapeDtypeStruct((rows * st, nv * patches), bf16),
        in_specs=[pl.BlockSpec(memory_space=pltpu.HBM)] * 4,
        out_specs=vmem,
        scratch_shapes=[
            pltpu.VMEM((rows, depth), bf16),
            pltpu.VMEM((rows, depth), bf16),
            pltpu.SMEM((4, rows), jnp.int32),
            pltpu.SMEM((rows,), f32),
            pltpu.VMEM((2, 2, nz, rows, depth), bf16),
            pltpu.VMEM((nb, rows, depth), bf16),
            pltpu.VMEM((nb, rows, wide), f32),
            pltpu.VMEM((nv, rows, wide), f32),
            pltpu.VMEM((nb * nl, rows, wide), f32),
            pltpu.VMEM((ITERS, 2 * nz, nb, wide), f32),
            pltpu.VMEM((nb, wide), f32),
            pltpu.VMEM((nl // 2 * nv, 2, st, width), bf16),
            pltpu.VMEM((nx * nl, 2, st, width), bf16),
            pltpu.VMEM((nv, st, width), bf16),
            pltpu.VMEM((nv, st, width), bf16),
            *sems,
        ],
        compiler_params=pltpu.CompilerParams(
            collective_id=0, has_side_effects=True, vmem_limit_bytes=VMEM
        ),
        name="couple",
    )(*[
        pltpu.with_memory_space_constraint(a, pltpu.HBM)
        for a in (latents, noise, offsets.reshape(rows, 4).T, times)
    ])
    made = jnp.dot(tokens, embed, preferred_element_type=f32).astype(bf16)
    return made.reshape(rows, st, embed.shape[1])


def solution(mesh):
    placed = (P("clip", "val"), P("clip", "val"), P("clip", None, None), P("clip"), P())
    return jax.shard_map(
        functools.partial(on_device, mesh.shape["clip"], mesh.shape["val"]),
        mesh=mesh,
        in_specs=placed,
        out_specs=P("clip", "val", None),
        check_vma=False,
    )
```

```python
import functools
import math

import jax
import jax.numpy as jnp
from jax import lax
from jax.experimental import pallas as pl
from jax.experimental.pallas import tpu as pltpu
from jax.sharding import PartitionSpec as P

P_SIZE = 64
FR = 2
GW = 16
GH = 4
ITERS = 4
VMEM = 16 << 20
S = FR * GH * GW
LOG2E = 1.4426950408889634


def ring(n):
    return sorted(range(1, n), key=lambda i: -min(i, n - i))


def turn(x, patches):
    return jnp.concatenate([x[:, p * S:(p + 1) * S] for p in range(patches)], axis=0).T


def couple(nz, nb, nv, lat_in, noise_in, off_in, times_in, out, lat, noise, off, times, pw, lg, part, rv, g, ex, urow, pb, rp, ms, la,
           w_s, w_r, l_s, l_r, w_far, r_s, r_r, g_s, g_r, e_s, e_r, c_s, c_r, a_s, a_r, p_s, p_r, i_s, f_s, f_r, k_s):
    nl, nx = nv // 2, nb // 2
    rows, depth = lat.shape
    patches = depth // S
    wide = nb * rows
    st = S // nv
    width = patches * rows
    clip = lax.axis_index("clip")
    v = lax.axis_index("val")
    z, b = clip // nb, lax.rem(clip, nb)
    h, x = b // nx, lax.rem(b, nx)
    l, k = v // 2, lax.rem(v, 2)
    y, ny = h * nl + l, 2 * nl
    nh = nz // 2
    zh, zl = z // nh, lax.rem(z, nh)
    left = []

    def at(z_, b_, v_):
        return {"clip": z_ * nb + b_, "val": v_}

    def send(src, dst, s_sem, r_sem, where):
        pltpu.make_async_remote_copy(src, dst, s_sem, r_sem, device_id=where).start()

    def came(like, sem):
        pltpu.make_async_remote_copy(like, like, sem, sem, device_id=at(z, b, v)).wait_recv()

    def gone(like, sem):
        left.append(lambda: pltpu.make_async_remote_copy(like, like, sem, sem, device_id=at(z, b, v)).wait_send())

    def finish():
        while left:
            left.pop()()

    z_peers = [lax.rem(z + i, nz) for i in ring(nz)]
    far = (1 - h) * nx + x
    near_peers = [h * nx + lax.rem(x + i, nx) for i in ring(nx)]
    l_others = [nl - 1 - l] if nl == 2 else [nl - 1 - l, lax.rem(l + 2, 4), l + 1 - 2 * lax.rem(l, 2)]
    v_peers = [lt * 2 + kt for lt in l_others for kt in (1 - k, k)] + [l * 2 + (1 - k)]

    barrier = pltpu.get_barrier_semaphore()
    for bt in [far] + near_peers:
        pl.semaphore_signal(barrier, inc=1, device_id=at(z, bt, v))
    for zt in z_peers:
        pl.semaphore_signal(barrier, inc=1, device_id=at(zt, b, v))
    for vt in v_peers:
        pl.semaphore_signal(barrier, inc=1, device_id=at(z, b, vt))

    loads = [
        pltpu.make_async_copy(src, dst, i_s.at[i])
        for i, (src, dst) in enumerate(((off_in, off), (noise_in, noise), (lat_in, lat), (times_in, times)))
    ]
    for load in loads:
        load.start()

    rowi = lax.broadcasted_iota(jnp.int32, (rows, S), 0)
    lane = lax.broadcasted_iota(jnp.int32, (rows, S), 1)
    first = lane < GH * GW
    sy = jnp.zeros((rows, S), jnp.int32)
    sx = jnp.zeros((rows, S), jnp.int32)
    loads[0].wait()
    for i in range(rows):
        here = rowi == i
        sy = jnp.where(here, jnp.where(first, off[0, i], off[2, i]), sy)
        sx = jnp.where(here, jnp.where(first, off[1, i], off[3, i]), sx)
    col = lane & (GW - 1)
    row = (lane // GW) & (GH - 1)
    loads[1].wait()
    for p in range(patches):
        t = noise[:, p * S:(p + 1) * S].astype(jnp.float32)
        for bit in (1, 2, 4, 8):
            turned = jnp.where(col >= bit, pltpu.roll(t, bit, 1), pltpu.roll(t, S - GW + bit, 1))
            t = jnp.where((sx & bit) != 0, turned, t)
        for bit in (1, 2):
            turned = jnp.where(
                row >= bit, pltpu.roll(t, bit * GW, 1), pltpu.roll(t, S - GH * GW + bit * GW, 1)
            )
            t = jnp.where((sy & bit) != 0, turned, t)
        pw[zh, k, b, :, p * S:(p + 1) * S] = t.astype(jnp.bfloat16)
    loads[2].wait()
    loads[3].wait()
    lg[z] = lat[...]
    pl.semaphore_wait(barrier, (nz - 1) + nx + (nv - 1))

    for zt in z_peers:
        send(lat, lg.at[z], l_s, l_r, at(zt, b, v))
    gone(lg.at[pl.ds(0, nz - 1)], l_s)
    mine = pw.at[zh, k, b]
    send(mine, mine, w_s, w_far, at(z, far, v))
    for bt in near_peers:
        send(mine, mine, w_s, w_r, at(z, bt, v))
    gone(pw.at[zh, k, pl.ds(0, nx)], w_s)

    ms[...] = turn(lat[...].astype(jnp.float32), patches).astype(jnp.bfloat16).reshape(nv, st, width)
    for vt in v_peers:
        send(ms.at[vt], la.at[v], a_s, a_r, at(z, b, vt))
    gone(ms.at[pl.ds(0, nv - 1)], a_s)
    la[v] = ms[v]
    came(mine, w_far)
    passed = pw.at[zh, k, far]
    for bt in near_peers:
        send(passed, passed, k_s, w_r, at(z, bt, v))
    gone(pw.at[zh, k, pl.ds(0, nx - 1)], k_s)
    came(lg.at[pl.ds(0, nz - 1)], l_r)
    came(pw.at[zh, k, pl.ds(0, 2 * (nx - 1))], w_r)
    neighbour = at(z, b, l * 2 + (1 - k))
    facing = at(lax.rem(z + nh, nz), b, v)
    panel = pw.at[zh, k]
    noises = pw[zh, k].reshape(wide, depth)
    square = noises.astype(jnp.float32)
    square = jnp.sum(square * square, axis=1, keepdims=True)
    diagonal = lax.broadcasted_iota(jnp.int32, (wide, wide), 0) == lax.broadcasted_iota(
        jnp.int32, (wide, wide), 1
    )
    square = jnp.sum(jnp.where(diagonal, square, 0.0), axis=0, keepdims=True)

    gram = lax.dot_general(
        lg[...].reshape(nz * rows, depth), noises, (((1,), (1,)), ((), ())), preferred_element_type=jnp.float32
    )
    part[...] = (square - 2.0 * gram).reshape(nz, rows, wide)
    for vt in v_peers:
        send(part.at[vt], rv.at[v], r_s, r_r, at(z, b, vt))
    gone(part.at[pl.ds(0, nv - 1)], r_s)
    rv[v] = part[v]
    came(rv.at[pl.ds(0, nv - 1)], r_r)
    volume = float(nv * depth)
    entropy = 0.5 / math.sqrt(volume)

    piece = g.at[z * ny + y]
    piece[...] = jnp.sum(rv[...], axis=0) * (LOG2E / (volume * entropy))

    def at_y(i):
        return at(z, i // nl * nx + x, lax.rem(i, nl) * 2 + k)

    y_peers = [lax.rem(y + i, ny) for i in ring(ny)]
    for i, yt, zt in zip(ring(nz), y_peers, z_peers):
        send(piece, piece, g_s, g_r.at[0, i], at_y(yt))
        send(piece, piece, g_s, g_r.at[1, i], at(zt, b, v))
    gone(g.at[pl.ds(0, ny - 1 + nz - 1)], g_s)
    for i in reversed(ring(nz)):
        yt, zt = lax.rem(y + ny - i, ny), lax.rem(z + nz - i, nz)
        came(piece, g_r.at[0, i])
        part_of = g.at[z * ny + yt, pl.ds(0, rows // 2)]
        for onward in z_peers:
            send(part_of, part_of, f_s, f_r, at(onward, b, v))
        came(piece, g_r.at[1, i])
        part_of = g.at[zt * ny + y, pl.ds(rows // 2, rows // 2)]
        for onward in y_peers:
            send(part_of, part_of, f_s, f_r, at_y(onward))
    pieces = g.at[pl.ds(0, (ny - 1) * (nz - 1))]
    gone(pieces, f_s)
    came(pieces, f_r)
    send(panel, panel, p_s.at[0], p_r.at[0], neighbour)
    gone(panel, p_s.at[0])
    send(panel, panel, p_s.at[1], p_r.at[1], facing)
    gone(panel, p_s.at[1])

    blocks = nz
    own_e = x * 2 + k

    def tile(c, first=0, count=ny):
        return g[pl.ds(c * ny + first, count)].reshape(count * rows, wide)

    def row_stats(dual, first=0, count=ny):
        top = dual[0:1] - tile(0, first, count)
        for c in range(1, blocks):
            top = jnp.maximum(top, dual[c:c + 1] - tile(c, first, count))
        top = jnp.max(top, axis=1, keepdims=True)
        total = jnp.exp2(dual[0:1] - tile(0, first, count) - top)
        for c in range(1, blocks):
            total = total + jnp.exp2(dual[c:c + 1] - tile(c, first, count) - top)
        return top, jnp.sum(total, axis=1, keepdims=True)

    e_peers = [(bt, kt) for bt in near_peers for kt in (1 - k, k)] + [(b, 1 - k)]

    dual = jnp.zeros((blocks, wide), jnp.float32)
    for it in range(ITERS):
        top, total = row_stats(dual)
        row_dual = -(top + jnp.log2(total))
        for c in range(blocks):
            t = row_dual - tile(c)
            top = jnp.max(t, axis=0, keepdims=True)
            total = jnp.sum(jnp.exp2(t - top), axis=0, keepdims=True)
            ex[it, own_e, c:c + 1] = top + jnp.log2(total)
        here = ex.at[it, own_e]

        for bt, kt in e_peers:
            send(here, here, e_s.at[it], e_r.at[it], at(z, bt, l * 2 + kt))
        others = ex.at[it, pl.ds(0, 2 * nx - 1)]
        gone(others, e_s.at[it])
        if it == ITERS - 1:
            passed = pw.at[1 - zh, k]
            came(passed, p_r.at[1])
            send(passed, passed, p_s.at[2], p_r.at[2], neighbour)
            gone(passed, p_s.at[2])
        came(others, e_r.at[it])
        parts = ex[it]
        top = jnp.max(parts, axis=0)
        total = jnp.sum(jnp.exp2(parts - top[None]), axis=0)
        dual = -(top + jnp.log2(total))

    urow[...] = dual
    count = nl // 2
    start = h * nl + zh * count
    top, total = row_stats(dual, start, count)
    weights = []
    for half in range(2):
        at_z = half * nh + zl
        t = urow[pl.ds(at_z, 1)] - g[pl.ds(at_z * ny + start, count)].reshape(count * rows, wide)
        weights.append((jnp.exp2(t - top) / total).astype(jnp.bfloat16))

    came(pw.at[zh, 1 - k], p_r.at[0])
    came(pw.at[1 - zh, 1 - k], p_r.at[2])
    parity = lax.rem(zl, 2)
    slot = l * nh + zl
    partial = []
    for kk in range(2):
        coupled = jnp.dot(weights[0], pw[0, kk].reshape(wide, depth), preferred_element_type=jnp.float32)
        partial.append(
            coupled + jnp.dot(weights[1], pw[1, kk].reshape(wide, depth), preferred_element_type=jnp.float32)
        )

    for i in range(count):
        for kk in range(2):
            made = turn(partial[kk][i * rows:(i + 1) * rows], patches).astype(jnp.bfloat16)
            pb[i * nv:(i + 1) * nv, kk] = made.reshape(nv, st, width)
        zt = 2 * i + k
        for vt in v_peers:
            send(pb.at[i * nv + vt], rp.at[slot], c_s, c_r.at[l], at(zh * nh + zt, b, vt))

        @pl.when(zt != zl)
        def _():
            send(pb.at[i * nv + v], rp.at[slot], c_s, c_r.at[l], at(zh * nh + zt, b, v))

    @pl.when(parity == k)
    def _():
        rp[slot] = pb[zl // 2 * nv + v]

    finish()
    lane = lax.broadcasted_iota(jnp.int32, (st, width), 1) & (rows - 1)
    time = jnp.zeros((st, width), jnp.float32)
    for i in range(rows):
        time = jnp.where(lane == i, times[i], time)
    clip_of = lax.broadcasted_iota(jnp.int32, (rows, st, width), 0)
    keep = (lax.broadcasted_iota(jnp.int32, (rows, st, width), 2) & (rows - 1)) == clip_of
    from_lane = lax.broadcasted_iota(jnp.int32, (width, nv * patches), 0) // rows
    to_patch = lax.broadcasted_iota(jnp.int32, (width, nv * patches), 1)
    came(la.at[pl.ds(0, nv - 1)], a_r)
    number = nh * nl
    made = jnp.zeros((rows * st, nv * patches), jnp.float32)
    for i, lt in enumerate([l] + l_others[::-1]):
        if i == 0:

            @pl.when(parity == k)
            def _():
                came(rp.at[pl.ds(0, nh - 1)], c_r.at[lt])

            @pl.when(parity != k)
            def _():
                came(rp.at[pl.ds(0, nh)], c_r.at[lt])

        else:
            came(rp.at[pl.ds(0, nh)], c_r.at[lt])
        for kk in range(2):
            coupled = rp[lt * nh, kk].astype(jnp.float32)
            for zt in range(1, nh):
                coupled = coupled + rp[lt * nh + zt, kk].astype(jnp.float32)
            mixed = (1.0 - time) * la[lt * 2 + kk].astype(jnp.float32) + time * coupled
            spread = jnp.where(keep, mixed[None], 0.0).reshape(rows * st, width).astype(jnp.bfloat16)
            start = (lt * 2 + kk) * patches
            pick = jnp.where(to_patch == from_lane + start, 1.0, 0.0).astype(jnp.bfloat16)
            made = made + jnp.dot(spread, pick, preferred_element_type=jnp.float32)
    out[...] = made.astype(jnp.bfloat16)

    @pl.when(parity == k)
    def _():
        gone(pb.at[pl.ds(0, number - 1)], c_s)
        finish()

    @pl.when(parity != k)
    def _():
        gone(pb, c_s)
        finish()


def on_device(nc, nv, latents, noise, offsets, times, embed):
    nb = nv
    nz, nl, nx = nc // nb, nv // 2, nb // 2
    rows, depth = latents.shape
    patches = depth // S
    st = S // nv
    nh = nz // 2
    wide = nb * rows
    width = patches * rows
    f32, bf16 = jnp.float32, jnp.bfloat16
    vmem = pl.BlockSpec(memory_space=pltpu.VMEM)
    sems = []
    for shape in ((), (), (), (), (), (), (), (), (2, nz), (ITERS,), (ITERS,), (), (nl,), (), (), (3,), (3,), (4,), (), (), ()):
        sems.append(pltpu.SemaphoreType.DMA(shape) if shape else pltpu.SemaphoreType.DMA)
    tokens = pl.pallas_call(
        functools.partial(couple, nz, nb, nv),
        out_shape=jax.ShapeDtypeStruct((rows * st, nv * patches), bf16),
        in_specs=[pl.BlockSpec(memory_space=pltpu.HBM)] * 4,
        out_specs=vmem,
        scratch_shapes=[
            pltpu.VMEM((rows, depth), bf16),
            pltpu.VMEM((rows, depth), bf16),
            pltpu.SMEM((4, rows), jnp.int32),
            pltpu.SMEM((rows,), f32),
            pltpu.VMEM((2, 2, nb, rows, depth), bf16),
            pltpu.VMEM((nz, rows, depth), bf16),
            pltpu.VMEM((nz, rows, wide), f32),
            pltpu.VMEM((nv, rows, wide), f32),
            pltpu.VMEM((nz * 2 * nl, rows, wide), f32),
            pltpu.VMEM((ITERS, 2 * nx, nz, wide), f32),
            pltpu.VMEM((nz, wide), f32),
            pltpu.VMEM((nl // 2 * nv, 2, st, width), bf16),
            pltpu.VMEM((nh * nl, 2, st, width), bf16),
            pltpu.VMEM((nv, st, width), bf16),
            pltpu.VMEM((nv, st, width), bf16),
            *sems,
        ],
        compiler_params=pltpu.CompilerParams(
            collective_id=0, has_side_effects=True, vmem_limit_bytes=VMEM
        ),
        name="couple",
    )(*[
        pltpu.with_memory_space_constraint(a, pltpu.HBM)
        for a in (latents, noise, offsets.reshape(rows, 4).T, times)
    ])
    made = jnp.dot(tokens, embed, preferred_element_type=f32).astype(bf16)
    return made.reshape(rows, st, embed.shape[1])


def solution(mesh):
    placed = (P("clip", "val"), P("clip", "val"), P("clip", None, None), P("clip"), P())
    return jax.shard_map(
        functools.partial(on_device, mesh.shape["clip"], mesh.shape["val"]),
        mesh=mesh,
        in_specs=placed,
        out_specs=P("clip", "val", None),
        check_vma=False,
    )
```

```python
import functools
import math

import jax
import jax.numpy as jnp
from jax import lax
from jax.experimental import pallas as pl
from jax.experimental.pallas import tpu as pltpu
from jax.sharding import PartitionSpec as P

P_SIZE = 64
FR = 2
GW = 16
GH = 4
ITERS = 4
VMEM = 16 << 20
S = FR * GH * GW
LOG2E = 1.4426950408889634


def ring(n):
    return sorted(range(1, n), key=lambda i: -min(i, n - i))


def turn(x, patches):
    return jnp.concatenate([x[:, p * S:(p + 1) * S] for p in range(patches)], axis=0).T


def couple(nz, nb, nv, lat_in, noise_in, off_in, times_in, out, lat, noise, off, times, pw, lg, part, rv, g, ex, urow, pb, rp, ms, la,
           w_s, w_r, l_s, l_r, w_far, r_s, r_r, g_s, g_r, e_s, e_r, c_s, c_r, a_s, a_r, p_s, p_r, i_s, f_s, f_r, k_s):
    nl, nx = nv // 2, nb // 2
    rows, depth = lat.shape
    patches = depth // S
    wide = nb * rows
    st = S // nv
    width = patches * rows
    clip = lax.axis_index("clip")
    v = lax.axis_index("val")
    z, b = clip // nb, lax.rem(clip, nb)
    h, x = b // nx, lax.rem(b, nx)
    l, k = v // 2, lax.rem(v, 2)
    y, ny = h * nl + l, 2 * nl
    nh = nz // 2
    zh, zl = z // nh, lax.rem(z, nh)
    left = []

    def at(z_, b_, v_):
        return {"clip": z_ * nb + b_, "val": v_}

    def send(src, dst, s_sem, r_sem, where):
        pltpu.make_async_remote_copy(src, dst, s_sem, r_sem, device_id=where).start()

    def came(like, sem):
        pltpu.make_async_remote_copy(like, like, sem, sem, device_id=at(z, b, v)).wait_recv()

    def gone(like, sem):
        left.append(lambda: pltpu.make_async_remote_copy(like, like, sem, sem, device_id=at(z, b, v)).wait_send())

    def finish():
        while left:
            left.pop()()

    z_peers = [lax.rem(z + i, nz) for i in ring(nz)]
    far = (1 - h) * nx + x
    near_peers = [h * nx + lax.rem(x + i, nx) for i in ring(nx)]
    l_others = [nl - 1 - l] if nl == 2 else [nl - 1 - l, lax.rem(l + 2, 4), l + 1 - 2 * lax.rem(l, 2)]
    v_peers = [lt * 2 + kt for lt in l_others for kt in (1 - k, k)] + [l * 2 + (1 - k)]

    barrier = pltpu.get_barrier_semaphore()
    for bt in [far] + near_peers:
        pl.semaphore_signal(barrier, inc=1, device_id=at(z, bt, v))
    for zt in z_peers:
        pl.semaphore_signal(barrier, inc=1, device_id=at(zt, b, v))
    for vt in v_peers:
        pl.semaphore_signal(barrier, inc=1, device_id=at(z, b, vt))

    loads = [
        pltpu.make_async_copy(src, dst, i_s.at[i])
        for i, (src, dst) in enumerate(((off_in, off), (noise_in, noise), (lat_in, lat), (times_in, times)))
    ]
    for load in loads:
        load.start()

    rowi = lax.broadcasted_iota(jnp.int32, (rows, S), 0)
    lane = lax.broadcasted_iota(jnp.int32, (rows, S), 1)
    first = lane < GH * GW
    sy = jnp.zeros((rows, S), jnp.int32)
    sx = jnp.zeros((rows, S), jnp.int32)
    loads[0].wait()
    for i in range(rows):
        here = rowi == i
        sy = jnp.where(here, jnp.where(first, off[0, i], off[2, i]), sy)
        sx = jnp.where(here, jnp.where(first, off[1, i], off[3, i]), sx)
    col = lane & (GW - 1)
    row = (lane // GW) & (GH - 1)
    loads[1].wait()
    for p in range(patches):
        t = noise[:, p * S:(p + 1) * S].astype(jnp.float32)
        for bit in (1, 2, 4, 8):
            turned = jnp.where(col >= bit, pltpu.roll(t, bit, 1), pltpu.roll(t, S - GW + bit, 1))
            t = jnp.where((sx & bit) != 0, turned, t)
        for bit in (1, 2):
            turned = jnp.where(
                row >= bit, pltpu.roll(t, bit * GW, 1), pltpu.roll(t, S - GH * GW + bit * GW, 1)
            )
            t = jnp.where((sy & bit) != 0, turned, t)
        pw[zh, k, b, :, p * S:(p + 1) * S] = t.astype(jnp.bfloat16)
    loads[2].wait()
    loads[3].wait()
    lg[z] = lat[...]
    pl.semaphore_wait(barrier, (nz - 1) + nx + (nv - 1))

    for zt in z_peers:
        send(lat, lg.at[z], l_s, l_r, at(zt, b, v))
    gone(lg.at[pl.ds(0, nz - 1)], l_s)
    mine = pw.at[zh, k, b]
    send(mine, mine, w_s, w_far, at(z, far, v))
    for bt in near_peers:
        send(mine, mine, w_s, w_r, at(z, bt, v))
    gone(pw.at[zh, k, pl.ds(0, nx)], w_s)

    ms[...] = turn(lat[...].astype(jnp.float32), patches).astype(jnp.bfloat16).reshape(nv, st, width)
    for vt in v_peers:
        send(ms.at[vt], la.at[v], a_s, a_r, at(z, b, vt))
    gone(ms.at[pl.ds(0, nv - 1)], a_s)
    la[v] = ms[v]
    came(mine, w_far)
    passed = pw.at[zh, k, far]
    for bt in near_peers:
        send(passed, passed, k_s, w_r, at(z, bt, v))
    gone(pw.at[zh, k, pl.ds(0, nx - 1)], k_s)
    came(lg.at[pl.ds(0, nz - 1)], l_r)
    came(pw.at[zh, k, pl.ds(0, 2 * (nx - 1))], w_r)
    neighbour = at(z, b, l * 2 + (1 - k))
    facing = at(lax.rem(z + nh, nz), b, v)
    panel = pw.at[zh, k]
    noises = pw[zh, k].reshape(wide, depth)
    square = noises.astype(jnp.float32)
    square = jnp.sum(square * square, axis=1, keepdims=True)
    diagonal = lax.broadcasted_iota(jnp.int32, (wide, wide), 0) == lax.broadcasted_iota(
        jnp.int32, (wide, wide), 1
    )
    square = jnp.sum(jnp.where(diagonal, square, 0.0), axis=0, keepdims=True)

    gram = lax.dot_general(
        lg[...].reshape(nz * rows, depth), noises, (((1,), (1,)), ((), ())), preferred_element_type=jnp.float32
    )
    part[...] = (square - 2.0 * gram).reshape(nz, rows, wide)
    for vt in v_peers:
        send(part.at[vt], rv.at[v], r_s, r_r, at(z, b, vt))
    gone(part.at[pl.ds(0, nv - 1)], r_s)
    rv[v] = part[v]
    came(rv.at[pl.ds(0, nv - 1)], r_r)
    volume = float(nv * depth)
    entropy = 0.5 / math.sqrt(volume)

    piece = g.at[z * ny + y]
    piece[...] = jnp.sum(rv[...], axis=0) * (LOG2E / (volume * entropy))

    def at_y(i):
        return at(z, i // nl * nx + x, lax.rem(i, nl) * 2 + k)

    y_peers = [lax.rem(y + i, ny) for i in ring(ny)]
    for i, yt, zt in zip(ring(nz), y_peers, z_peers):
        send(piece, piece, g_s, g_r.at[0, i], at_y(yt))
        send(piece, piece, g_s, g_r.at[1, i], at(zt, b, v))
    gone(g.at[pl.ds(0, ny - 1 + nz - 1)], g_s)
    for i in reversed(ring(nz)):
        yt, zt = lax.rem(y + ny - i, ny), lax.rem(z + nz - i, nz)
        came(piece, g_r.at[0, i])
        whole = g.at[z * ny + yt]
        for j, onward in zip(ring(nz), z_peers):
            if (i + j) % 2 == 0:
                send(whole, whole, f_s, f_r, at(onward, b, v))
        came(piece, g_r.at[1, i])
        whole = g.at[zt * ny + y]
        for j, onward in zip(ring(ny), y_peers):
            if (i + j) % 2:
                send(whole, whole, f_s, f_r, at_y(onward))
    pieces = g.at[pl.ds(0, (ny - 1) * (nz - 1))]
    gone(pieces, f_s)
    came(pieces, f_r)
    send(panel, panel, p_s.at[0], p_r.at[0], neighbour)
    gone(panel, p_s.at[0])
    send(panel, panel, p_s.at[1], p_r.at[1], facing)
    gone(panel, p_s.at[1])

    blocks = nz
    own_e = x * 2 + k

    def tile(c, first=0, count=ny):
        return g[pl.ds(c * ny + first, count)].reshape(count * rows, wide)

    def row_stats(dual, first=0, count=ny):
        top = dual[0:1] - tile(0, first, count)
        for c in range(1, blocks):
            top = jnp.maximum(top, dual[c:c + 1] - tile(c, first, count))
        top = jnp.max(top, axis=1, keepdims=True)
        total = jnp.exp2(dual[0:1] - tile(0, first, count) - top)
        for c in range(1, blocks):
            total = total + jnp.exp2(dual[c:c + 1] - tile(c, first, count) - top)
        return top, jnp.sum(total, axis=1, keepdims=True)

    e_peers = [(bt, kt) for bt in near_peers for kt in (1 - k, k)] + [(b, 1 - k)]

    dual = jnp.zeros((blocks, wide), jnp.float32)
    for it in range(ITERS):
        top, total = row_stats(dual)
        row_dual = -(top + jnp.log2(total))
        for c in range(blocks):
            t = row_dual - tile(c)
            top = jnp.max(t, axis=0, keepdims=True)
            total = jnp.sum(jnp.exp2(t - top), axis=0, keepdims=True)
            ex[it, own_e, c:c + 1] = top + jnp.log2(total)
        here = ex.at[it, own_e]

        for bt, kt in e_peers:
            send(here, here, e_s.at[it], e_r.at[it], at(z, bt, l * 2 + kt))
        others = ex.at[it, pl.ds(0, 2 * nx - 1)]
        gone(others, e_s.at[it])
        if it == ITERS - 1:
            passed = pw.at[1 - zh, k]
            came(passed, p_r.at[1])
            send(passed, passed, p_s.at[2], p_r.at[2], neighbour)
            gone(passed, p_s.at[2])
        came(others, e_r.at[it])
        parts = ex[it]
        top = jnp.max(parts, axis=0)
        total = jnp.sum(jnp.exp2(parts - top[None]), axis=0)
        dual = -(top + jnp.log2(total))

    urow[...] = dual
    count = nl // 2
    start = h * nl + zh * count
    top, total = row_stats(dual, start, count)
    weights = []
    for half in range(2):
        at_z = half * nh + zl
        t = urow[pl.ds(at_z, 1)] - g[pl.ds(at_z * ny + start, count)].reshape(count * rows, wide)
        weights.append((jnp.exp2(t - top) / total).astype(jnp.bfloat16))

    came(pw.at[zh, 1 - k], p_r.at[0])
    came(pw.at[1 - zh, 1 - k], p_r.at[2])
    parity = lax.rem(zl, 2)
    slot = l * nh + zl
    partial = []
    for kk in range(2):
        coupled = jnp.dot(weights[0], pw[0, kk].reshape(wide, depth), preferred_element_type=jnp.float32)
        partial.append(
            coupled + jnp.dot(weights[1], pw[1, kk].reshape(wide, depth), preferred_element_type=jnp.float32)
        )

    for i in range(count):
        for kk in range(2):
            made = turn(partial[kk][i * rows:(i + 1) * rows], patches).astype(jnp.bfloat16)
            pb[i * nv:(i + 1) * nv, kk] = made.reshape(nv, st, width)
        zt = 2 * i + k
        for vt in v_peers:
            send(pb.at[i * nv + vt], rp.at[slot], c_s, c_r.at[l], at(zh * nh + zt, b, vt))

        @pl.when(zt != zl)
        def _():
            send(pb.at[i * nv + v], rp.at[slot], c_s, c_r.at[l], at(zh * nh + zt, b, v))

    @pl.when(parity == k)
    def _():
        rp[slot] = pb[zl // 2 * nv + v]

    finish()
    lane = lax.broadcasted_iota(jnp.int32, (st, width), 1) & (rows - 1)
    time = jnp.zeros((st, width), jnp.float32)
    for i in range(rows):
        time = jnp.where(lane == i, times[i], time)
    clip_of = lax.broadcasted_iota(jnp.int32, (rows, st, width), 0)
    keep = (lax.broadcasted_iota(jnp.int32, (rows, st, width), 2) & (rows - 1)) == clip_of
    from_lane = lax.broadcasted_iota(jnp.int32, (width, nv * patches), 0) // rows
    to_patch = lax.broadcasted_iota(jnp.int32, (width, nv * patches), 1)
    came(la.at[pl.ds(0, nv - 1)], a_r)
    number = nh * nl
    made = jnp.zeros((rows * st, nv * patches), jnp.float32)
    for i, lt in enumerate([l] + l_others[::-1]):
        if i == 0:

            @pl.when(parity == k)
            def _():
                came(rp.at[pl.ds(0, nh - 1)], c_r.at[lt])

            @pl.when(parity != k)
            def _():
                came(rp.at[pl.ds(0, nh)], c_r.at[lt])

        else:
            came(rp.at[pl.ds(0, nh)], c_r.at[lt])
        for kk in range(2):
            coupled = rp[lt * nh, kk].astype(jnp.float32)
            for zt in range(1, nh):
                coupled = coupled + rp[lt * nh + zt, kk].astype(jnp.float32)
            mixed = (1.0 - time) * la[lt * 2 + kk].astype(jnp.float32) + time * coupled
            spread = jnp.where(keep, mixed[None], 0.0).reshape(rows * st, width).astype(jnp.bfloat16)
            start = (lt * 2 + kk) * patches
            pick = jnp.where(to_patch == from_lane + start, 1.0, 0.0).astype(jnp.bfloat16)
            made = made + jnp.dot(spread, pick, preferred_element_type=jnp.float32)
    out[...] = made.astype(jnp.bfloat16)

    @pl.when(parity == k)
    def _():
        gone(pb.at[pl.ds(0, number - 1)], c_s)
        finish()

    @pl.when(parity != k)
    def _():
        gone(pb, c_s)
        finish()


def on_device(nc, nv, latents, noise, offsets, times, embed):
    nb = nv
    nz, nl, nx = nc // nb, nv // 2, nb // 2
    rows, depth = latents.shape
    patches = depth // S
    st = S // nv
    nh = nz // 2
    wide = nb * rows
    width = patches * rows
    f32, bf16 = jnp.float32, jnp.bfloat16
    vmem = pl.BlockSpec(memory_space=pltpu.VMEM)
    sems = []
    for shape in ((), (), (), (), (), (), (), (), (2, nz), (ITERS,), (ITERS,), (), (nl,), (), (), (3,), (3,), (4,), (), (), ()):
        sems.append(pltpu.SemaphoreType.DMA(shape) if shape else pltpu.SemaphoreType.DMA)
    tokens = pl.pallas_call(
        functools.partial(couple, nz, nb, nv),
        out_shape=jax.ShapeDtypeStruct((rows * st, nv * patches), bf16),
        in_specs=[pl.BlockSpec(memory_space=pltpu.HBM)] * 4,
        out_specs=vmem,
        scratch_shapes=[
            pltpu.VMEM((rows, depth), bf16),
            pltpu.VMEM((rows, depth), bf16),
            pltpu.SMEM((4, rows), jnp.int32),
            pltpu.SMEM((rows,), f32),
            pltpu.VMEM((2, 2, nb, rows, depth), bf16),
            pltpu.VMEM((nz, rows, depth), bf16),
            pltpu.VMEM((nz, rows, wide), f32),
            pltpu.VMEM((nv, rows, wide), f32),
            pltpu.VMEM((nz * 2 * nl, rows, wide), f32),
            pltpu.VMEM((ITERS, 2 * nx, nz, wide), f32),
            pltpu.VMEM((nz, wide), f32),
            pltpu.VMEM((nl // 2 * nv, 2, st, width), bf16),
            pltpu.VMEM((nh * nl, 2, st, width), bf16),
            pltpu.VMEM((nv, st, width), bf16),
            pltpu.VMEM((nv, st, width), bf16),
            *sems,
        ],
        compiler_params=pltpu.CompilerParams(
            collective_id=0, has_side_effects=True, vmem_limit_bytes=VMEM
        ),
        name="couple",
    )(*[
        pltpu.with_memory_space_constraint(a, pltpu.HBM)
        for a in (latents, noise, offsets.reshape(rows, 4).T, times)
    ])
    made = jnp.dot(tokens, embed, preferred_element_type=f32).astype(bf16)
    return made.reshape(rows, st, embed.shape[1])


def solution(mesh):
    placed = (P("clip", "val"), P("clip", "val"), P("clip", None, None), P("clip"), P())
    return jax.shard_map(
        functools.partial(on_device, mesh.shape["clip"], mesh.shape["val"]),
        mesh=mesh,
        in_specs=placed,
        out_specs=P("clip", "val", None),
        check_vma=False,
    )
```

```python
import functools
import math

import jax
import jax.numpy as jnp
from jax import lax
from jax.experimental import pallas as pl
from jax.experimental.pallas import tpu as pltpu
from jax.sharding import PartitionSpec as P

P_SIZE = 64
FR = 2
GW = 16
GH = 4
ITERS = 4
VMEM = 16 << 20
S = FR * GH * GW
LOG2E = 1.4426950408889634


def ring(n):
    return sorted(range(1, n), key=lambda i: -min(i, n - i))


def along_y_first(i, j, n):
    by_y, by_z = min(i, n - i), min(j, n - j)
    return by_y > by_z or (by_y == by_z and (i + j) % n == 0)


def turn(x, patches):
    return jnp.concatenate([x[:, p * S:(p + 1) * S] for p in range(patches)], axis=0).T


def couple(nz, nb, nv, lat_in, noise_in, off_in, times_in, out, lat, noise, off, times, pw, lg, part, rv, g, ex, urow, pb, rp, ms, la,
           w_s, w_r, l_s, l_r, w_far, r_s, r_r, g_s, g_r, e_s, e_r, c_s, c_r, a_s, a_r, p_s, p_r, i_s, f_s, f_r, k_s):
    nl, nx = nv // 2, nb // 2
    rows, depth = lat.shape
    patches = depth // S
    wide = nb * rows
    st = S // nv
    width = patches * rows
    clip = lax.axis_index("clip")
    v = lax.axis_index("val")
    z, b = clip // nb, lax.rem(clip, nb)
    h, x = b // nx, lax.rem(b, nx)
    l, k = v // 2, lax.rem(v, 2)
    y, ny = h * nl + l, 2 * nl
    nh = nz // 2
    zh, zl = z // nh, lax.rem(z, nh)
    left = []

    def at(z_, b_, v_):
        return {"clip": z_ * nb + b_, "val": v_}

    def send(src, dst, s_sem, r_sem, where):
        pltpu.make_async_remote_copy(src, dst, s_sem, r_sem, device_id=where).start()

    def came(like, sem):
        pltpu.make_async_remote_copy(like, like, sem, sem, device_id=at(z, b, v)).wait_recv()

    def gone(like, sem):
        left.append(lambda: pltpu.make_async_remote_copy(like, like, sem, sem, device_id=at(z, b, v)).wait_send())

    def finish():
        while left:
            left.pop()()

    z_peers = [lax.rem(z + i, nz) for i in ring(nz)]
    far = (1 - h) * nx + x
    near_peers = [h * nx + lax.rem(x + i, nx) for i in ring(nx)]
    l_others = [nl - 1 - l] if nl == 2 else [nl - 1 - l, lax.rem(l + 2, 4), l + 1 - 2 * lax.rem(l, 2)]
    v_peers = [lt * 2 + kt for lt in l_others for kt in (1 - k, k)] + [l * 2 + (1 - k)]

    barrier = pltpu.get_barrier_semaphore()
    for bt in [far] + near_peers:
        pl.semaphore_signal(barrier, inc=1, device_id=at(z, bt, v))
    for zt in z_peers:
        pl.semaphore_signal(barrier, inc=1, device_id=at(zt, b, v))
    for vt in v_peers:
        pl.semaphore_signal(barrier, inc=1, device_id=at(z, b, vt))

    loads = [
        pltpu.make_async_copy(src, dst, i_s.at[i])
        for i, (src, dst) in enumerate(((off_in, off), (noise_in, noise), (lat_in, lat), (times_in, times)))
    ]
    for load in loads:
        load.start()

    rowi = lax.broadcasted_iota(jnp.int32, (rows, S), 0)
    lane = lax.broadcasted_iota(jnp.int32, (rows, S), 1)
    first = lane < GH * GW
    sy = jnp.zeros((rows, S), jnp.int32)
    sx = jnp.zeros((rows, S), jnp.int32)
    loads[0].wait()
    for i in range(rows):
        here = rowi == i
        sy = jnp.where(here, jnp.where(first, off[0, i], off[2, i]), sy)
        sx = jnp.where(here, jnp.where(first, off[1, i], off[3, i]), sx)
    col = lane & (GW - 1)
    row = (lane // GW) & (GH - 1)
    loads[1].wait()
    for p in range(patches):
        t = noise[:, p * S:(p + 1) * S].astype(jnp.float32)
        for bit in (1, 2, 4, 8):
            turned = jnp.where(col >= bit, pltpu.roll(t, bit, 1), pltpu.roll(t, S - GW + bit, 1))
            t = jnp.where((sx & bit) != 0, turned, t)
        for bit in (1, 2):
            turned = jnp.where(
                row >= bit, pltpu.roll(t, bit * GW, 1), pltpu.roll(t, S - GH * GW + bit * GW, 1)
            )
            t = jnp.where((sy & bit) != 0, turned, t)
        pw[zh, k, b, :, p * S:(p + 1) * S] = t.astype(jnp.bfloat16)
    loads[2].wait()
    loads[3].wait()
    lg[z] = lat[...]
    pl.semaphore_wait(barrier, (nz - 1) + nx + (nv - 1))

    mine = pw.at[zh, k, b]
    send(mine, mine, w_s, w_far, at(z, far, v))
    for bt in near_peers:
        send(mine, mine, w_s, w_r, at(z, bt, v))
    gone(pw.at[zh, k, pl.ds(0, nx)], w_s)
    for zt in z_peers:
        send(lat, lg.at[z], l_s, l_r, at(zt, b, v))
    gone(lg.at[pl.ds(0, nz - 1)], l_s)

    ms[...] = turn(lat[...].astype(jnp.float32), patches).astype(jnp.bfloat16).reshape(nv, st, width)
    for vt in v_peers:
        send(ms.at[vt], la.at[v], a_s, a_r, at(z, b, vt))
    gone(ms.at[pl.ds(0, nv - 1)], a_s)
    la[v] = ms[v]
    came(mine, w_far)
    passed = pw.at[zh, k, far]
    for bt in near_peers:
        send(passed, passed, k_s, w_r, at(z, bt, v))
    gone(pw.at[zh, k, pl.ds(0, nx - 1)], k_s)
    came(lg.at[pl.ds(0, nz - 1)], l_r)
    came(pw.at[zh, k, pl.ds(0, 2 * (nx - 1))], w_r)
    neighbour = at(z, b, l * 2 + (1 - k))
    facing = at(lax.rem(z + nh, nz), b, v)
    panel = pw.at[zh, k]
    noises = pw[zh, k].reshape(wide, depth)
    square = noises.astype(jnp.float32)
    square = jnp.sum(square * square, axis=1, keepdims=True)
    diagonal = lax.broadcasted_iota(jnp.int32, (wide, wide), 0) == lax.broadcasted_iota(
        jnp.int32, (wide, wide), 1
    )
    square = jnp.sum(jnp.where(diagonal, square, 0.0), axis=0, keepdims=True)

    gram = lax.dot_general(
        lg[...].reshape(nz * rows, depth), noises, (((1,), (1,)), ((), ())), preferred_element_type=jnp.float32
    )
    part[...] = (square - 2.0 * gram).reshape(nz, rows, wide)
    for vt in v_peers:
        send(part.at[vt], rv.at[v], r_s, r_r, at(z, b, vt))
    gone(part.at[pl.ds(0, nv - 1)], r_s)
    rv[v] = part[v]
    came(rv.at[pl.ds(0, nv - 1)], r_r)
    volume = float(nv * depth)
    entropy = 0.5 / math.sqrt(volume)

    piece = g.at[z * ny + y]
    piece[...] = jnp.sum(rv[...], axis=0) * (LOG2E / (volume * entropy))

    def at_y(i):
        return at(z, i // nl * nx + x, lax.rem(i, nl) * 2 + k)

    y_peers = [lax.rem(y + i, ny) for i in ring(ny)]
    for i, yt, zt in zip(ring(nz), y_peers, z_peers):
        send(piece, piece, g_s, g_r.at[0, i], at_y(yt))
        send(piece, piece, g_s, g_r.at[1, i], at(zt, b, v))
    gone(g.at[pl.ds(0, ny - 1 + nz - 1)], g_s)
    for i in reversed(ring(nz)):
        yt, zt = lax.rem(y + ny - i, ny), lax.rem(z + nz - i, nz)
        came(piece, g_r.at[0, i])
        whole = g.at[z * ny + yt]
        for j, onward in zip(ring(nz), z_peers):
            if along_y_first(i, j, ny):
                send(whole, whole, f_s, f_r, at(onward, b, v))
        came(piece, g_r.at[1, i])
        whole = g.at[zt * ny + y]
        for j, onward in zip(ring(ny), y_peers):
            if not along_y_first(j, i, ny):
                send(whole, whole, f_s, f_r, at_y(onward))
    pieces = g.at[pl.ds(0, (ny - 1) * (nz - 1))]
    gone(pieces, f_s)
    came(pieces, f_r)
    send(panel, panel, p_s.at[0], p_r.at[0], neighbour)
    gone(panel, p_s.at[0])
    send(panel, panel, p_s.at[1], p_r.at[1], facing)
    gone(panel, p_s.at[1])

    blocks = nz
    own_e = x * 2 + k

    def tile(c, first=0, count=ny):
        return g[pl.ds(c * ny + first, count)].reshape(count * rows, wide)

    def row_stats(dual, first=0, count=ny):
        top = dual[0:1] - tile(0, first, count)
        for c in range(1, blocks):
            top = jnp.maximum(top, dual[c:c + 1] - tile(c, first, count))
        top = jnp.max(top, axis=1, keepdims=True)
        total = jnp.exp2(dual[0:1] - tile(0, first, count) - top)
        for c in range(1, blocks):
            total = total + jnp.exp2(dual[c:c + 1] - tile(c, first, count) - top)
        return top, jnp.sum(total, axis=1, keepdims=True)

    e_peers = [(bt, kt) for bt in near_peers for kt in (1 - k, k)] + [(b, 1 - k)]

    dual = jnp.zeros((blocks, wide), jnp.float32)
    for it in range(ITERS):
        top, total = row_stats(dual)
        row_dual = -(top + jnp.log2(total))
        for c in range(blocks):
            t = row_dual - tile(c)
            top = jnp.max(t, axis=0, keepdims=True)
            total = jnp.sum(jnp.exp2(t - top), axis=0, keepdims=True)
            ex[it, own_e, c:c + 1] = top + jnp.log2(total)
        here = ex.at[it, own_e]

        for bt, kt in e_peers:
            send(here, here, e_s.at[it], e_r.at[it], at(z, bt, l * 2 + kt))
        others = ex.at[it, pl.ds(0, 2 * nx - 1)]
        gone(others, e_s.at[it])
        if it == ITERS - 1:
            passed = pw.at[1 - zh, k]
            came(passed, p_r.at[1])
            send(passed, passed, p_s.at[2], p_r.at[2], neighbour)
            gone(passed, p_s.at[2])
        came(others, e_r.at[it])
        parts = ex[it]
        top = jnp.max(parts, axis=0)
        total = jnp.sum(jnp.exp2(parts - top[None]), axis=0)
        dual = -(top + jnp.log2(total))

    urow[...] = dual
    count = nl // 2
    start = h * nl + zh * count
    top, total = row_stats(dual, start, count)
    weights = []
    for half in range(2):
        at_z = half * nh + zl
        t = urow[pl.ds(at_z, 1)] - g[pl.ds(at_z * ny + start, count)].reshape(count * rows, wide)
        weights.append((jnp.exp2(t - top) / total).astype(jnp.bfloat16))

    came(pw.at[zh, 1 - k], p_r.at[0])
    came(pw.at[1 - zh, 1 - k], p_r.at[2])
    parity = lax.rem(zl, 2)
    slot = l * nh + zl
    partial = []
    for kk in range(2):
        coupled = jnp.dot(weights[0], pw[0, kk].reshape(wide, depth), preferred_element_type=jnp.float32)
        partial.append(
            coupled + jnp.dot(weights[1], pw[1, kk].reshape(wide, depth), preferred_element_type=jnp.float32)
        )

    for i in range(count):
        for kk in range(2):
            made = turn(partial[kk][i * rows:(i + 1) * rows], patches).astype(jnp.bfloat16)
            pb[i * nv:(i + 1) * nv, kk] = made.reshape(nv, st, width)
        zt = 2 * i + k
        for vt in v_peers:
            send(pb.at[i * nv + vt], rp.at[slot], c_s, c_r.at[l], at(zh * nh + zt, b, vt))

        @pl.when(zt != zl)
        def _():
            send(pb.at[i * nv + v], rp.at[slot], c_s, c_r.at[l], at(zh * nh + zt, b, v))

    @pl.when(parity == k)
    def _():
        rp[slot] = pb[zl // 2 * nv + v]

    finish()
    lane = lax.broadcasted_iota(jnp.int32, (st, width), 1) & (rows - 1)
    time = jnp.zeros((st, width), jnp.float32)
    for i in range(rows):
        time = jnp.where(lane == i, times[i], time)
    clip_of = lax.broadcasted_iota(jnp.int32, (rows, st, width), 0)
    keep = (lax.broadcasted_iota(jnp.int32, (rows, st, width), 2) & (rows - 1)) == clip_of
    from_lane = lax.broadcasted_iota(jnp.int32, (width, nv * patches), 0) // rows
    to_patch = lax.broadcasted_iota(jnp.int32, (width, nv * patches), 1)
    came(la.at[pl.ds(0, nv - 1)], a_r)
    number = nh * nl
    made = jnp.zeros((rows * st, nv * patches), jnp.float32)
    for i, lt in enumerate([l] + l_others[::-1]):
        if i == 0:

            @pl.when(parity == k)
            def _():
                came(rp.at[pl.ds(0, nh - 1)], c_r.at[lt])

            @pl.when(parity != k)
            def _():
                came(rp.at[pl.ds(0, nh)], c_r.at[lt])

        else:
            came(rp.at[pl.ds(0, nh)], c_r.at[lt])
        for kk in range(2):
            coupled = rp[lt * nh, kk].astype(jnp.float32)
            for zt in range(1, nh):
                coupled = coupled + rp[lt * nh + zt, kk].astype(jnp.float32)
            mixed = (1.0 - time) * la[lt * 2 + kk].astype(jnp.float32) + time * coupled
            spread = jnp.where(keep, mixed[None], 0.0).reshape(rows * st, width).astype(jnp.bfloat16)
            start = (lt * 2 + kk) * patches
            pick = jnp.where(to_patch == from_lane + start, 1.0, 0.0).astype(jnp.bfloat16)
            made = made + jnp.dot(spread, pick, preferred_element_type=jnp.float32)
    out[...] = made.astype(jnp.bfloat16)

    @pl.when(parity == k)
    def _():
        gone(pb.at[pl.ds(0, number - 1)], c_s)
        finish()

    @pl.when(parity != k)
    def _():
        gone(pb, c_s)
        finish()


def on_device(nc, nv, latents, noise, offsets, times, embed):
    nb = nv
    nz, nl, nx = nc // nb, nv // 2, nb // 2
    rows, depth = latents.shape
    patches = depth // S
    st = S // nv
    nh = nz // 2
    wide = nb * rows
    width = patches * rows
    f32, bf16 = jnp.float32, jnp.bfloat16
    vmem = pl.BlockSpec(memory_space=pltpu.VMEM)
    sems = []
    for shape in ((), (), (), (), (), (), (), (), (2, nz), (ITERS,), (ITERS,), (), (nl,), (), (), (3,), (3,), (4,), (), (), ()):
        sems.append(pltpu.SemaphoreType.DMA(shape) if shape else pltpu.SemaphoreType.DMA)
    tokens = pl.pallas_call(
        functools.partial(couple, nz, nb, nv),
        out_shape=jax.ShapeDtypeStruct((rows * st, nv * patches), bf16),
        in_specs=[pl.BlockSpec(memory_space=pltpu.HBM)] * 4,
        out_specs=vmem,
        scratch_shapes=[
            pltpu.VMEM((rows, depth), bf16),
            pltpu.VMEM((rows, depth), bf16),
            pltpu.SMEM((4, rows), jnp.int32),
            pltpu.SMEM((rows,), f32),
            pltpu.VMEM((2, 2, nb, rows, depth), bf16),
            pltpu.VMEM((nz, rows, depth), bf16),
            pltpu.VMEM((nz, rows, wide), f32),
            pltpu.VMEM((nv, rows, wide), f32),
            pltpu.VMEM((nz * 2 * nl, rows, wide), f32),
            pltpu.VMEM((ITERS, 2 * nx, nz, wide), f32),
            pltpu.VMEM((nz, wide), f32),
            pltpu.VMEM((nl // 2 * nv, 2, st, width), bf16),
            pltpu.VMEM((nh * nl, 2, st, width), bf16),
            pltpu.VMEM((nv, st, width), bf16),
            pltpu.VMEM((nv, st, width), bf16),
            *sems,
        ],
        compiler_params=pltpu.CompilerParams(
            collective_id=0, has_side_effects=True, vmem_limit_bytes=VMEM
        ),
        name="couple",
    )(*[
        pltpu.with_memory_space_constraint(a, pltpu.HBM)
        for a in (latents, noise, offsets.reshape(rows, 4).T, times)
    ])
    made = jnp.dot(tokens, embed, preferred_element_type=f32).astype(bf16)
    return made.reshape(rows, st, embed.shape[1])


def solution(mesh):
    placed = (P("clip", "val"), P("clip", "val"), P("clip", None, None), P("clip"), P())
    return jax.shard_map(
        functools.partial(on_device, mesh.shape["clip"], mesh.shape["val"]),
        mesh=mesh,
        in_specs=placed,
        out_specs=P("clip", "val", None),
        check_vma=False,
    )
```
